32 devices in a mesh: comp: 2 (over core), gx: 4 (over y, x), gy: 4 (over z).
Axes of the slice: x: 2, y: 2, z: 4, core: 2. Of those that a mesh axis runs over, the one named last changes fastest.
Arguments:
- state: float32 [2, 8, 96, 3072], P('comp', None, 'gx', 'gy'), may hold values from -6 to 6
- response: float32 [2, 8, 3072], P('comp'), may hold values from -0.95 to 0
- diffusion: float32 [2, 96, 3072], P('comp', 'gx', 'gy'), may hold values from 0.02 to 0.24
- land_mask: int32 [96, 3072], P('gx', 'gy'), may hold values 0 or 1
- couple_src: int32 [2, 4, 4, 16, 128], P('comp', 'gx', 'gy'), may hold values from 0 to 18431
- couple_dst: int32 [2, 4, 4, 16, 128], P('comp', 'gx', 'gy'), may hold values from 0 to 18431
- couple_weight: float32 [2, 4, 4, 16, 128], P('comp', 'gx', 'gy'), may hold values from 0.1 to 1
- couple_count: int32 [2, 4, 4, 16], P('comp', 'gx', 'gy'), may hold values from 0 to 128, as said below
Outputs:
- final_state: float32 [2, 8, 96, 3072], P('comp', None, 'gx', 'gy')
The draws below stay inside these ranges and needn't reach their ends.
Inputs may be any that keep to these rules, and one draw needn't show every extreme that they name: `couple_count`: at most 128 live slots per ordered device pair; every sending device has one pair with exactly 128.
All inputs are finite; a program needn't handle non-finite values. No bound on the sum of `land_mask` on one device may be relied on, other than what follows from the above.
Results may differ from the reference program's by a relative error of at most 0.0095.
Values may be sent and summed in bfloat16 or wider, within the bound.
A program may use at most 128 MiB of HBM per device.

```python
import math
import jax
import jax.numpy as jnp
from jax import lax

LEV = 8
FC = 4
STEPS = 1
RD = 24
COLS = 3072
CAP = 128
CD = 768
ROWS = 96
NPEER = 16
N_GX = 4
N_GY = 4


def draw_couple_count(key, part):
    key_a = jax.random.fold_in(key, 11)
    key_b = jax.random.fold_in(key, 12)
    key_c = jax.random.fold_in(key, 13)
    first = jax.random.randint(key_a, (2, N_GX, N_GY, NPEER), 0, CAP + 1)
    second = jax.random.randint(key_b, (2, N_GX, N_GY, NPEER), 0, CAP + 1)
    counts = jnp.maximum(first, second)
    chosen = jax.random.randint(key_c, (2, N_GX, N_GY, 1), 0, NPEER)
    peers = jnp.arange(NPEER, dtype=jnp.int32)[None, None, None, :]
    return jnp.where(peers == chosen, CAP, counts).astype(jnp.int32)


def place_ends(drawn, own_key, smallest, largest):
    longest = drawn.shape.index(max(drawn.shape))
    spots = []
    for shift in (0, 1):
        where = [jax.random.randint(jax.random.fold_in(own_key, axis), (), 0, length) for axis, length in enumerate(drawn.shape)]
        where[longest] = (where[longest] + shift) % drawn.shape[longest]
        spots.append(tuple(where))
    return drawn.at[spots[0]].set(smallest).at[spots[1]].set(largest)


def levels(own_key, dims, cuts, low, largest):
    gain, own = 1.0, jax.random.fold_in(own_key, 6)
    for axis_at, blocks in cuts:
        heights = jnp.exp(jax.random.uniform(jax.random.fold_in(own, axis_at), (blocks,), jnp.float32, low / len(cuts), largest / len(cuts)))
        gain = gain * jnp.repeat(heights, dims[axis_at] // blocks).reshape([-1 if axis == axis_at else 1 for axis in range(len(dims))])
    return gain


def centred(rng, extent, width, limit, split=(), held_as=jnp.bfloat16):
    level = levels(rng, extent, split, -0.22, 0.18) if split else 1.0
    drawn = jax.random.normal(rng, extent, jnp.float32) * width * level
    return jnp.minimum(jnp.maximum(drawn, -limit), limit).astype(held_as)


def setup_inputs(seed: int = 0) -> dict:
    keys = jax.random.split(jax.random.key(seed), 9)
    return {
        "state": centred(keys[0], (2, LEV, ROWS, COLS), 1.0, 6.0, ((0, 2), (2, 4), (3, 4)), jnp.float32),
        "response": jnp.clip(-0.95 + 0.95 * jax.random.uniform(keys[1], (2, LEV, COLS), jnp.float32) ** levels(keys[1], (2, LEV, COLS), ((0, 2),), -0.2, 0.2), -0.95, 0.0),
        "diffusion": jnp.clip(jnp.exp(math.log(0.24) - 2.4849066 * jax.random.uniform(keys[2], (2, ROWS, COLS), jnp.float32) ** levels(keys[2], (2, ROWS, COLS), ((0, 2), (1, 4), (2, 4)), -0.2, 0.2)), 0.02, 0.24),
        "land_mask": place_ends((jax.random.randint(keys[3], (ROWS, COLS), 0, 4) < 3).astype(jnp.int32), jax.random.fold_in(keys[3], 1), 0, 1),
        "couple_src": place_ends(jax.random.randint(keys[4], (2, N_GX, N_GY, NPEER, CAP), 0, RD * CD), jax.random.fold_in(keys[4], 1), 0, (RD * CD) - 1).astype(jnp.int32),
        "couple_dst": place_ends(jax.random.randint(keys[5], (2, N_GX, N_GY, NPEER, CAP), 0, RD * CD), jax.random.fold_in(keys[5], 1), 0, (RD * CD) - 1).astype(jnp.int32),
        "couple_weight": jnp.clip(0.1 + 0.9 * jax.random.uniform(keys[6], (2, N_GX, N_GY, NPEER, CAP), jnp.float32) ** levels(keys[6], (2, N_GX, N_GY, NPEER, CAP), ((0, 2), (1, 4), (2, 4)), -0.2, 0.2), 0.1, 1.0),
        "couple_count": draw_couple_count(jax.random.fold_in(keys[8], 71), 0),
    }


def make_table(cols):
    rows_idx = jnp.arange(cols, dtype=jnp.int32)[:, None]
    wave_idx = jnp.arange(cols // 2, dtype=jnp.int32)[None, :]
    phase = (rows_idx * wave_idx) % cols
    angle = phase.astype(jnp.float32) * (2.0 * math.pi / cols)
    return jnp.concatenate([jnp.cos(angle), jnp.sin(angle)], axis=1).astype(jnp.bfloat16)


def reference(state, response, diffusion, land_mask, couple_src, couple_dst, couple_weight, couple_count):
    cells = RD * CD
    table = make_table(COLS)
    slot_idx = jnp.arange(CAP, dtype=jnp.int32)
    live = slot_idx[None, None, None, None, :] < couple_count[..., None]
    weights = jnp.where(live, couple_weight, jnp.float32(0.0)).reshape(2, NPEER, NPEER, CAP)
    src_idx = couple_src.reshape(2, NPEER, NPEER * CAP)
    dst_idx = couple_dst.reshape(2, NPEER, NPEER * CAP)
    keep = jnp.stack([jnp.ones((ROWS, COLS), jnp.float32), land_mask.astype(jnp.float32)])
    lead = jnp.arange(2 * FC * NPEER, dtype=jnp.int32).reshape(2, FC, NPEER, 1)
    global_idx = (lead * cells + dst_idx[:, None, :, :]).reshape(-1)
    for step in range(STEPS):
        surface = state[:, :FC].reshape(2, FC, N_GX, RD, N_GY, CD)
        blocks = surface.transpose(0, 1, 2, 4, 3, 5).reshape(2, FC, NPEER, cells)
        values = jnp.take_along_axis(blocks, jnp.broadcast_to(src_idx[:, None], (2, FC, NPEER, NPEER * CAP)), axis=3)
        values = values.reshape(2, FC, NPEER, NPEER, CAP) * weights[:, None]
        arrived = values[::-1].transpose(0, 1, 3, 2, 4).reshape(-1)
        updated = blocks.reshape(-1).at[global_idx].add(arrived)
        updated = updated.reshape(2, FC, N_GX, N_GY, RD, CD).transpose(0, 1, 2, 4, 3, 5).reshape(2, FC, ROWS, COLS)
        state = jnp.concatenate([updated, state[:, FC:]], axis=1)
        grid_bf = state.astype(jnp.bfloat16).reshape(-1, COLS)
        spec = jnp.dot(grid_bf, table, preferred_element_type=jnp.float32).reshape(2, LEV, ROWS, COLS)
        filtered = (spec * response[:, :, None, :]).astype(jnp.bfloat16).reshape(-1, COLS)
        incr = lax.dot_general(filtered, table, (((1,), (1,)), ((), ())), preferred_element_type=jnp.float32)
        incr = (incr * (2.0 / COLS)).astype(jnp.bfloat16).reshape(2, LEV, ROWS, COLS)
        state = state + incr.astype(jnp.float32)
        padded = jnp.pad(state, ((0, 0), (0, 0), (1, 1), (0, 0)))
        state = state + diffusion[:, None] * (padded[:, :, 2:] + padded[:, :, :-2] - 2.0 * state)
        state = state * keep[:, None]
    return state
```

```python
import functools
import math

import jax
import jax.numpy as jnp
import ml_dtypes
import numpy as np
from jax import lax
from jax.experimental import pallas as pl
from jax.experimental.pallas import tpu as pltpu
from jax.sharding import PartitionSpec as P

FC = 4
LANES = 128
CHUNK = 256
MESH = pl.DeviceIdType.MESH
F32 = jnp.float32
BF16 = jnp.bfloat16


def lane_tables(cols):
    blocks = cols // LANES
    lane = np.arange(LANES)[:, None]
    step = np.arange(LANES // 2)[None, :]
    tables = np.zeros((blocks // 2, 2 * LANES, 2 * LANES), np.float64)
    for k in range(blocks // 2):
        for place, residue in enumerate((k, blocks - k) if k else (0, blocks // 2)):
            angle = 2.0 * math.pi / cols * (lane * (blocks * step + residue) % cols)
            cos, sin = np.cos(angle), np.sin(angle)
            span = slice(place * LANES, (place + 1) * LANES)
            if k:
                sign = -1.0 if place else 1.0
                tables[k, :LANES, span] = np.concatenate([cos, sin], axis=1)
                tables[k, LANES:, span] = np.concatenate([-sin, cos], axis=1) * sign
            else:
                tables[k, span, span] = np.concatenate([cos, sin], axis=1)
    return tables.astype(ml_dtypes.bfloat16)


def weighted(terms):
    total = None
    for coef, value in terms:
        if abs(coef) < 1e-12:
            continue
        if abs(abs(coef) - 1.0) < 1e-12:
            if total is None:
                total = value if coef > 0 else -value
            else:
                total = total + value if coef > 0 else total - value
        else:
            scaled = value * np.float32(coef)
            total = scaled if total is None else total + scaled
    return total


def block_forward(x):
    n = len(x)
    half, quarter = n // 2, n // 4
    cos = lambda a, k: math.cos(2.0 * math.pi * (a * k % n) / n)
    sin = lambda a, k: math.sin(2.0 * math.pi * (a * k % n) / n)
    even = {a: x[a] + x[n - a] for a in range(1, half)}
    odd = {a: x[a] - x[n - a] for a in range(1, half)}
    even[0], even[half] = x[0], x[half]
    ee = {a: even[a] + even[half - a] for a in range(quarter)}
    eo = {a: even[a] - even[half - a] for a in range(quarter)}
    ee[quarter] = even[quarter]
    oe = {a: odd[a] - odd[half - a] for a in range(1, quarter)}
    oo = {a: odd[a] + odd[half - a] for a in range(1, quarter)}
    oo[quarter] = odd[quarter]
    p, q = {}, {}
    for k in range(half + 1):
        p[k] = weighted([(cos(a, k), v) for a, v in (eo if k % 2 else ee).items()])
        if 0 < k < half:
            q[k] = weighted([(sin(a, k), v) for a, v in (oo if k % 2 else oe).items()])
    return p, q


def block_backward(p, q):
    half = max(p)
    n, quarter = 2 * half, half // 2
    cos = lambda a, k: math.cos(2.0 * math.pi * (a * k % n) / n)
    sin = lambda a, k: math.sin(2.0 * math.pi * (a * k % n) / n)
    u, v = {}, {}
    for a in range(quarter + 1):
        ue = weighted([(cos(a, k), p[k]) for k in range(0, half + 1, 2)])
        uo = weighted([(cos(a, k), p[k]) for k in range(1, half + 1, 2)])
        if a == quarter:
            u[a] = ue
        else:
            u[a], u[half - a] = ue + uo, ue - uo
        if a:
            vo = weighted([(sin(a, k), q[k]) for k in range(1, half, 2)])
            if a == quarter:
                v[a] = vo
            else:
                ve = weighted([(sin(a, k), q[k]) for k in range(2, half, 2)])
                v[a], v[half - a] = vo + ve, vo - ve
    x = [None] * n
    x[0], x[half] = u[0], u[half]
    for a in range(1, half):
        x[a], x[n - a] = u[a] + v[a], u[a] - v[a]
    return x


def flipped(index, mask, size):
    total, bit = 0, 1
    while bit < size:
        digit = (index // bit) % 2
        total = total + bit * (1 - digit if mask & bit else digit)
        bit *= 2
    return total


def far_first(size):
    return sorted(range(1, size), key=lambda mask: (mask < size // 2, mask))


def phases(levels, groups_y):
    if FC % groups_y == 0 and (levels - FC) % groups_y == 0:
        return [(FC, levels), (0, FC)]
    return [(0, levels)]


def kernel(
    gx, gy, state_ref, resp_ref, rate_ref, land_ref, src_ref, dst_ref, weight_ref, count_ref, table_ref,
    out_ref,
    fields, outv, table, resp, rate, land, sendc, recvc, onehot,
    fsend, frecv, bsend, brecv, edges, halos,
    load_sem, out_sem, csend_sem, crecv_sem, fsend_sem, frecv_sem, bsend_sem, brecv_sem, hsend_sem, hrecv_sem,
):
    levels, rows, cols = fields.shape
    peers, _, slots = sendc.shape
    nb = cols // LANES
    lines = nb * rows
    padded = fsend.shape[-2]
    blocks = nb * gy
    pieces = phases(levels, gy)
    section = lax.axis_index("comp")
    g = lax.axis_index("gx")
    h = lax.axis_index("gy")
    me = g * gy + h
    right, left = (g + 1) % gx, (g + gx - 1) % gx

    def load(source, target, at):
        copy = pltpu.make_async_copy(source, target, load_sem.at[at])
        copy.start()
        return copy

    load_low = load(state_ref.at[pl.ds(0, FC)], fields.at[pl.ds(0, FC)], 0)
    load_high = load(state_ref.at[pl.ds(FC, levels - FC)], fields.at[pl.ds(FC, levels - FC)], 1)
    load_table = load(table_ref, table, 2)
    load_resp = load(resp_ref, resp, 3)
    load_rate = load(rate_ref, rate, 4)
    load_land = load(land_ref, land, 5)

    barrier = pltpu.get_barrier_semaphore()
    for mask in far_first(gy):
        pl.semaphore_signal(barrier, inc=1, device_id={"gy": flipped(h, mask, gy)}, device_id_type=MESH)
    for side in (right, left):
        pl.semaphore_signal(barrier, inc=1, device_id={"gx": side}, device_id_type=MESH)

    @pl.loop(0, peers)
    def _(q):
        pl.semaphore_signal(
            barrier, inc=1, device_id={"comp": 1 - section, "gx": q // gy, "gy": q % gy}, device_id_type=MESH
        )

    def pack(level):
        values = fields[level]
        tall = jnp.concatenate([values[:, i * LANES : (i + 1) * LANES] for i in range(nb)], axis=0)
        if padded > lines:
            tall = jnp.concatenate([tall, jnp.zeros((padded - lines, LANES), F32)], axis=0)
        return tall.astype(BF16)

    def exchange(source, target, send_sem, recv_sem, piece, j):
        copies = []
        for mask in far_first(gy):
            other = flipped(h, mask, gy)
            copy = pltpu.make_async_remote_copy(
                src_ref=source.at[piece, j, other],
                dst_ref=target.at[piece, j, h],
                send_sem=send_sem.at[piece, j, mask],
                recv_sem=recv_sem.at[piece, j, mask],
                device_id={"gy": other},
                device_id_type=MESH,
            )
            copy.start()
            copies.append(copy)
        target[piece, j, h] = source[piece, j, h]
        return copies

    def send_forward(piece):
        low, high = pieces[piece]
        copies = []
        for j in range((high - low) // gy):
            for owner in range(gy):
                fsend[piece, j, owner] = pack(low + j * gy + owner)
            copies += exchange(fsend, frecv, fsend_sem, frecv_sem, piece, j)
        return copies

    def transform(piece, copies):
        low, high = pieces[piece]
        for copy in copies:
            copy.wait_recv()
        sent = []
        for j in range((high - low) // gy):
            level = low + j * gy + h
            x = []
            for source in range(gy):
                tall = frecv[piece, j, source].astype(F32)
                x += [tall[i * rows : (i + 1) * rows] for i in range(nb)]
            p, q = block_forward(x)
            pz, qz = {}, {}
            for k in range(blocks // 2):
                first, second = (p[k], q[k]) if k else (p[0], p[blocks // 2])
                mates = (k, blocks - k) if k else (0, blocks // 2)
                y = jnp.concatenate([first, second], axis=1).astype(BF16)
                spec = jnp.dot(y, table[k], preferred_element_type=F32)
                gain = jnp.concatenate([resp[level, pl.ds(m, 1), :] for m in mates], axis=1)
                filtered = (spec * gain).astype(BF16)
                z = lax.dot_general(filtered, table[k], (((1,), (1,)), ((), ())), preferred_element_type=F32)
                pz[k] = z[:, :LANES]
                if k:
                    qz[k] = z[:, LANES:]
                else:
                    pz[blocks // 2] = z[:, LANES:]
            back = block_backward(pz, qz)
            for owner in range(gy):
                tall = jnp.concatenate(back[owner * nb : (owner + 1) * nb], axis=0)
                if padded > lines:
                    tall = jnp.concatenate([tall, jnp.zeros((padded - lines, LANES), F32)], axis=0)
                bsend[piece, j, owner] = tall.astype(BF16)
            sent += exchange(bsend, brecv, bsend_sem, brecv_sem, piece, j)
        return sent

    def add_increments(piece, copies):
        low, high = pieces[piece]
        for copy in copies:
            copy.wait_recv()
        for j in range((high - low) // gy):
            for owner in range(gy):
                tall = brecv[piece, j, owner].astype(F32)
                wide = jnp.concatenate([tall[i * rows : (i + 1) * rows] for i in range(nb)], axis=1)
                level = low + j * gy + owner
                updated = fields[level] + wide
                fields[level] = updated
                edges[0, pl.ds(level, 1), :] = updated[:1]
                edges[1, pl.ds(level, 1), :] = updated[rows - 1 :]
        span = pl.ds(low, high - low)
        halo = []
        for way, side in ((0, left), (1, right)):
            copy = pltpu.make_async_remote_copy(
                src_ref=edges.at[way, span],
                dst_ref=halos.at[way, span],
                send_sem=hsend_sem.at[piece, way],
                recv_sem=hrecv_sem.at[piece, way],
                device_id={"gx": side},
                device_id_type=MESH,
            )
            copy.start()
            halo.append(copy)
        return halo

    def finish(piece, halo):
        low, high = pieces[piece]
        for copy in halo:
            copy.wait_recv()
        keep = jnp.where(section == 1, land[...].astype(F32), 1.0)
        row = lax.broadcasted_iota(jnp.int32, (rows, cols), 0)
        above = jnp.where(g == gx - 1, 0.0, 1.0)
        below = jnp.where(g == 0, 0.0, 1.0)
        writes = []
        for level in range(low, high):
            values = fields[level]
            after = jnp.where(row == rows - 1, halos[0, pl.ds(level, 1), :] * above, pltpu.roll(values, rows - 1, 0))
            before = jnp.where(row == 0, halos[1, pl.ds(level, 1), :] * below, pltpu.roll(values, 1, 0))
            outv[level] = (values + rate[...] * (after + before - 2.0 * values)) * keep
        span = pl.ds(low, high - low)
        write = pltpu.make_async_copy(outv.at[span], out_ref.at[span], out_sem.at[piece])
        write.start()
        return write

    def cells(index):
        row = ((index.astype(F32) + 0.5) * np.float32(1.0 / cols)).astype(jnp.int32)
        return row, index - row * cols

    per = CHUNK // slots
    load_low.wait()
    surface = fields[pl.ds(0, FC)].reshape(FC * rows, cols).astype(BF16)

    @pl.loop(0, peers // per)
    def _(c):
        base = c * per
        index = jnp.concatenate([src_ref[pl.ds(base + i, 1), :] for i in range(per)], axis=1)
        row, col = cells(index)
        pick = jnp.where(lax.broadcasted_iota(jnp.int32, (cols, CHUNK), 0) == col, 1.0, 0.0).astype(BF16)
        found = jnp.dot(surface, pick, preferred_element_type=F32).reshape(FC, rows, CHUNK)
        mine = (lax.broadcasted_iota(jnp.int32, (rows, CHUNK), 0) == row)[None]
        values = jnp.sum(jnp.where(mine, found, 0.0), axis=1)
        for i in range(per):
            slot = lax.broadcasted_iota(jnp.int32, (1, slots), 1)
            weight = jnp.where(slot < count_ref[base + i], weight_ref[pl.ds(base + i, 1), :], 0.0)
            sendc[base + i] = values[:, i * slots : (i + 1) * slots] * weight

    pl.semaphore_wait(barrier, gy - 1 + 2 + peers)

    def couple_copy(q):
        return pltpu.make_async_remote_copy(
            src_ref=sendc.at[q],
            dst_ref=recvc.at[me],
            send_sem=csend_sem,
            recv_sem=crecv_sem,
            device_id={"comp": 1 - section, "gx": q // gy, "gy": q % gy},
            device_id_type=MESH,
        )

    @pl.loop(0, peers)
    def _(q):
        couple_copy(q).start()

    load_high.wait()
    forward = {}
    if len(pieces) == 2:
        forward[0] = send_forward(0)

    @pl.loop(0, peers // per)
    def _(c):
        base = c * per
        index = jnp.concatenate([dst_ref[pl.ds(base + i, 1), :] for i in range(per)], axis=1)
        _, col = cells(index)
        hot = jnp.where(lax.broadcasted_iota(jnp.int32, (cols, CHUNK), 0) == col, 1.0, 0.0)
        onehot[c] = hot.astype(BF16)

    everything = pltpu.make_async_remote_copy(
        src_ref=sendc, dst_ref=recvc, send_sem=csend_sem, recv_sem=crecv_sem,
        device_id={"comp": 1 - section}, device_id_type=MESH,
    )
    everything.wait_recv()

    def spread_chunk(c, total):
        base = c * per
        index = jnp.concatenate([dst_ref[pl.ds(base + i, 1), :] for i in range(per)], axis=1)
        row, _ = cells(index)
        mine = lax.broadcasted_iota(jnp.int32, (rows, CHUNK), 0) == row
        values = jnp.concatenate([recvc[base + i] for i in range(per)], axis=1)
        spread = jnp.concatenate([jnp.where(mine, values[c4 : c4 + 1], 0.0) for c4 in range(FC)], axis=0)
        return total + lax.dot_general(
            spread.astype(BF16), onehot[c], (((1,), (1,)), ((), ())), preferred_element_type=F32
        )

    added = lax.fori_loop(0, peers // per, spread_chunk, jnp.zeros((FC * rows, cols), F32))
    fields[pl.ds(0, FC)] = fields[pl.ds(0, FC)] + added.reshape(FC, rows, cols)

    last = len(pieces) - 1
    forward[last] = send_forward(last)
    load_table.wait()
    load_resp.wait()
    backward = {piece: transform(piece, forward[piece]) for piece in range(len(pieces))}
    load_rate.wait()
    load_land.wait()
    halo = {piece: add_increments(piece, backward[piece]) for piece in range(len(pieces))}
    writes = [finish(piece, halo[piece]) for piece in range(len(pieces))]
    everything.wait_send()
    for piece in range(len(pieces)):
        for copy in forward[piece] + backward[piece] + halo[piece]:
            copy.wait_send()
    for write in writes:
        write.wait()


def local(state, response, diffusion, land_mask, couple_src, couple_dst, couple_weight, couple_count):
    levels, rows, cols = state.shape[1:]
    gx, gy = lax.axis_size("gx"), lax.axis_size("gy")
    peers, slots = couple_src.shape[3:]
    cols_all = cols * gy
    blocks = cols_all // LANES
    pieces = phases(levels, gy)
    per_piece = (pieces[0][1] - pieces[0][0]) // gy
    padded = -(-(cols // LANES * rows) // 16) * 16
    tables = jnp.asarray(lane_tables(cols_all))
    resp = response[0].reshape(levels, 2, LANES // 2, blocks)
    resp = (jnp.transpose(resp, (0, 3, 1, 2)) * (2.0 / cols_all)).reshape(levels, blocks, LANES)
    anywhere = pl.BlockSpec(memory_space=pl.ANY)
    vmem = pl.BlockSpec(memory_space=pltpu.VMEM)
    smem = pl.BlockSpec(memory_space=pltpu.SMEM)
    message = (len(pieces), per_piece, gy, padded, LANES)
    dma = pltpu.SemaphoreType.DMA
    out = pl.pallas_call(
        functools.partial(kernel, gx, gy),
        out_shape=jax.ShapeDtypeStruct((levels, rows, cols), F32),
        in_specs=[anywhere] * 4 + [vmem] * 3 + [smem, anywhere],
        out_specs=anywhere,
        scratch_shapes=[
            pltpu.VMEM((levels, rows, cols), F32),
            pltpu.VMEM((levels, rows, cols), F32),
            pltpu.VMEM(tables.shape, BF16),
            pltpu.VMEM(resp.shape, F32),
            pltpu.VMEM((rows, cols), F32),
            pltpu.VMEM((rows, cols), jnp.int32),
            pltpu.VMEM((peers, FC, slots), F32),
            pltpu.VMEM((peers, FC, slots), F32),
            pltpu.VMEM((peers * slots // CHUNK, cols, CHUNK), BF16),
            pltpu.VMEM(message, BF16),
            pltpu.VMEM(message, BF16),
            pltpu.VMEM(message, BF16),
            pltpu.VMEM(message, BF16),
            pltpu.VMEM((2, levels, cols), F32),
            pltpu.VMEM((2, levels, cols), F32),
            dma((6,)),
            dma((len(pieces),)),
            dma,
            dma,
            dma(message[:3]),
            dma(message[:3]),
            dma(message[:3]),
            dma(message[:3]),
            dma((len(pieces), 2)),
            dma((len(pieces), 2)),
        ],
        compiler_params=pltpu.CompilerParams(
            collective_id=0, has_side_effects=True, vmem_limit_bytes=48 * 1024 * 1024
        ),
    )(
        state[0],
        resp,
        diffusion[0],
        land_mask,
        couple_src.reshape(peers, slots),
        couple_dst.reshape(peers, slots),
        couple_weight.reshape(peers, slots),
        couple_count.reshape(peers),
        tables,
    )
    return out[None]


def solution(mesh):
    return jax.shard_map(
        local,
        mesh=mesh,
        in_specs=(
            P("comp", None, "gx", "gy"),
            P("comp", None, None),
            P("comp", "gx", "gy"),
            P("gx", "gy"),
            P("comp", "gx", "gy", None, None),
            P("comp", "gx", "gy", None, None),
            P("comp", "gx", "gy", None, None),
            P("comp", "gx", "gy", None),
        ),
        out_specs=P("comp", None, "gx", "gy"),
        check_vma=False,
    )
```

```python
import functools
import math

import jax
import jax.numpy as jnp
import ml_dtypes
import numpy as np
from jax import lax
from jax.experimental import pallas as pl
from jax.experimental.pallas import tpu as pltpu
from jax.sharding import PartitionSpec as P

FC = 4
LANES = 128
CHUNK = 256
MESH = pl.DeviceIdType.MESH
F32 = jnp.float32
BF16 = jnp.bfloat16


def lane_tables(cols):
    blocks = cols // LANES
    lane = np.arange(LANES)[:, None]
    step = np.arange(LANES // 2)[None, :]
    tables = np.zeros((blocks // 2, 2 * LANES, 2 * LANES), np.float64)
    for k in range(blocks // 2):
        for place, residue in enumerate((k, blocks - k) if k else (0, blocks // 2)):
            angle = 2.0 * math.pi / cols * (lane * (blocks * step + residue) % cols)
            cos, sin = np.cos(angle), np.sin(angle)
            span = slice(place * LANES, (place + 1) * LANES)
            if k:
                sign = -1.0 if place else 1.0
                tables[k, :LANES, span] = np.concatenate([cos, sin], axis=1)
                tables[k, LANES:, span] = np.concatenate([-sin, cos], axis=1) * sign
            else:
                tables[k, span, span] = np.concatenate([cos, sin], axis=1)
    return tables.astype(ml_dtypes.bfloat16)


def pair_order(blocks):
    order = [0, blocks // 2]
    for k in range(1, blocks // 2):
        order += [k, blocks - k]
    return order


def spread_table(blocks):
    table = np.zeros((blocks * 16, blocks * LANES), np.float32)
    for place, residue in enumerate(pair_order(blocks)):
        for lane in range(LANES):
            table[blocks * (lane % 16) + residue, place * LANES + lane] = 1.0
    return table.astype(ml_dtypes.bfloat16)


def weighted(terms):
    total = None
    for coef, value in terms:
        if abs(coef) < 1e-12:
            continue
        if abs(abs(coef) - 1.0) < 1e-12:
            if total is None:
                total = value if coef > 0 else -value
            else:
                total = total + value if coef > 0 else total - value
        else:
            scaled = value * np.float32(coef)
            total = scaled if total is None else total + scaled
    return total


def block_forward(x):
    n = len(x)
    half, quarter = n // 2, n // 4
    cos = lambda a, k: math.cos(2.0 * math.pi * (a * k % n) / n)
    sin = lambda a, k: math.sin(2.0 * math.pi * (a * k % n) / n)
    even = {a: x[a] + x[n - a] for a in range(1, half)}
    odd = {a: x[a] - x[n - a] for a in range(1, half)}
    even[0], even[half] = x[0], x[half]
    ee = {a: even[a] + even[half - a] for a in range(quarter)}
    eo = {a: even[a] - even[half - a] for a in range(quarter)}
    ee[quarter] = even[quarter]
    oe = {a: odd[a] - odd[half - a] for a in range(1, quarter)}
    oo = {a: odd[a] + odd[half - a] for a in range(1, quarter)}
    oo[quarter] = odd[quarter]
    p, q = {}, {}
    for k in range(half + 1):
        p[k] = weighted([(cos(a, k), v) for a, v in (eo if k % 2 else ee).items()])
        if 0 < k < half:
            q[k] = weighted([(sin(a, k), v) for a, v in (oo if k % 2 else oe).items()])
    return p, q


def block_backward(p, q):
    half = max(p)
    n, quarter = 2 * half, half // 2
    cos = lambda a, k: math.cos(2.0 * math.pi * (a * k % n) / n)
    sin = lambda a, k: math.sin(2.0 * math.pi * (a * k % n) / n)
    u, v = {}, {}
    for a in range(quarter + 1):
        ue = weighted([(cos(a, k), p[k]) for k in range(0, half + 1, 2)])
        uo = weighted([(cos(a, k), p[k]) for k in range(1, half + 1, 2)])
        if a == quarter:
            u[a] = ue
        else:
            u[a], u[half - a] = ue + uo, ue - uo
        if a:
            vo = weighted([(sin(a, k), q[k]) for k in range(1, half, 2)])
            if a == quarter:
                v[a] = vo
            else:
                ve = weighted([(sin(a, k), q[k]) for k in range(2, half, 2)])
                v[a], v[half - a] = vo + ve, vo - ve
    x = [None] * n
    x[0], x[half] = u[0], u[half]
    for a in range(1, half):
        x[a], x[n - a] = u[a] + v[a], u[a] - v[a]
    return x


def flipped(index, mask, size):
    total, bit = 0, 1
    while bit < size:
        digit = (index // bit) % 2
        total = total + bit * (1 - digit if mask & bit else digit)
        bit *= 2
    return total


def far_first(size):
    return sorted(range(1, size), key=lambda mask: (mask < size // 2, mask))


def phases(levels, groups_y):
    if FC % groups_y == 0 and (levels - FC) % groups_y == 0:
        return [(FC, levels), (0, FC)]
    return [(0, levels)]


def kernel(
    gx, gy, state_hbm, resp_hbm, rate_hbm, land_hbm, src_hbm, dst_hbm, weight_hbm, count_hbm, table_hbm, place_hbm,
    out_ref,
    fields, outv, table, place, resp, gains, rate, land, src_ref, dst_ref, weight_ref, count_ref,
    sendc, recvc, dsts, landed, fsend, frecv, bsend, brecv, esend, erecv, edges, halos,
    load_sem, out_sem, csend_sem, crecv_sem, isend_sem, irecv_sem, fsend_sem, frecv_sem, bsend_sem, brecv_sem,
    esend_sem, erecv_sem, hsend_sem, hrecv_sem,
):
    levels, rows, cols = fields.shape
    peers, slots = src_ref.shape
    nb = cols // LANES
    lines = nb * rows
    padded = fsend.shape[-2]
    blocks = nb * gy
    pieces = phases(levels, gy)
    last = len(pieces) - 1
    section = lax.axis_index("comp")
    g = lax.axis_index("gx")
    h = lax.axis_index("gy")
    me = g * gy + h
    right, left = (g + 1) % gx, (g + gx - 1) % gx

    def load(source, target, at):
        copy = pltpu.make_async_copy(source, target, load_sem.at[at])
        copy.start()
        return copy

    load_high = load(state_hbm.at[pl.ds(FC, levels - FC)], fields.at[pl.ds(FC, levels - FC)], 4)
    load_low = load(state_hbm.at[pl.ds(0, FC)], fields.at[pl.ds(0, FC)], 0)
    load_dst = load(dst_hbm, dst_ref, 5)
    load_src = load(src_hbm, src_ref, 1)
    load_weight = load(weight_hbm, weight_ref, 2)
    load_count = load(count_hbm, count_ref, 3)
    load_place = load(place_hbm, place, 6)
    load_resp = load(resp_hbm, resp, 7)
    load_table = load(table_hbm, table, 8)
    load_rate = load(rate_hbm, rate, 9)
    load_land = load(land_hbm, land, 10)

    barrier = pltpu.get_barrier_semaphore()
    for mask in far_first(gy):
        pl.semaphore_signal(barrier, inc=1, device_id={"gy": flipped(h, mask, gy)}, device_id_type=MESH)
    for side in (right, left):
        pl.semaphore_signal(barrier, inc=1, device_id={"gx": side}, device_id_type=MESH)

    @pl.loop(0, peers)
    def _(q):
        pl.semaphore_signal(
            barrier, inc=1, device_id={"comp": 1 - section, "gx": q // gy, "gy": q % gy}, device_id_type=MESH
        )

    def filled(tall, count):
        if count > tall.shape[0]:
            tall = jnp.concatenate([tall, jnp.zeros((count - tall.shape[0], LANES), F32)], axis=0)
        return tall

    def pack(level):
        values = fields[level]
        tall = jnp.concatenate([values[:, i * LANES : (i + 1) * LANES] for i in range(nb)], axis=0)
        return filled(tall, padded).astype(BF16)

    def along_y(source, target, send_sem, recv_sem, mask):
        return pltpu.make_async_remote_copy(
            src_ref=source,
            dst_ref=target,
            send_sem=send_sem,
            recv_sem=recv_sem,
            device_id={"gy": flipped(h, mask, gy)},
            device_id_type=MESH,
        )

    def exchange(source, target, send_sem, recv_sem, *at):
        copies = {}
        for mask in far_first(gy):
            copies[mask] = along_y(
                source.at[(*at, flipped(h, mask, gy))],
                target.at[(*at, h)],
                send_sem.at[(*at, mask)],
                recv_sem.at[(*at, mask)],
                mask,
            )
            copies[mask].start()
        target[(*at, h)] = source[(*at, h)]
        return copies

    def counts(piece):
        low, high = pieces[piece]
        return range((high - low) // gy)

    def pack_piece(piece):
        for j in counts(piece):
            for owner in range(gy):
                fsend[piece, j, owner] = pack(pieces[piece][0] + j * gy + owner)

    def send_forward(piece):
        return [exchange(fsend, frecv, fsend_sem, frecv_sem, piece, j) for j in counts(piece)]

    def expand_gains():
        groups, width = LANES // 16, blocks * 16
        rows_all = []
        for piece, (low, high) in enumerate(pieces):
            for j in counts(piece):
                line = resp[pl.ds(low + j * gy + h, 1), :] * np.float32(2.0 / (groups * width))
                rows_all.append(jnp.concatenate([line[:, i * width : (i + 1) * width] for i in range(groups)], axis=0))
        values = jnp.concatenate(rows_all, axis=0)
        count = values.shape[0]
        top = values.astype(BF16)
        rest = (values - top.astype(F32)).astype(BF16)
        both = jnp.concatenate([top, rest], axis=0)
        lane = lax.broadcasted_iota(jnp.int32, (groups, 2 * LANES), 1) % LANES
        mine = lane // 16 == lax.broadcasted_iota(jnp.int32, (groups, 2 * LANES), 0)
        for k in range(blocks // 2):
            span = pl.ds(k * 2 * LANES, 2 * LANES)
            wide = jnp.dot(both, place[:, span], preferred_element_type=F32)
            wide = wide[:count] + wide[count:]
            at = 0
            for piece in range(len(pieces)):
                for j in counts(piece):
                    mixed = jnp.where(mine, wide[at : at + groups], 0.0)
                    gains[piece, j, :, span] = jnp.sum(mixed, axis=0, keepdims=True)
                    at += groups

    def transform(piece, arriving):
        sent = []
        for j in counts(piece):
            for copy in arriving[j].values():
                copy.wait_recv()
            x = []
            for source in range(gy):
                tall = frecv[piece, j, source].astype(F32)[:lines]
                if piece == last and j == 0:
                    tall = tall + landed[source]
                x += [tall[i * rows : (i + 1) * rows] for i in range(nb)]
            p, q = block_forward(x)
            pz, qz = {}, {}
            for k in range(blocks // 2):
                first, second = (p[k], q[k]) if k else (p[0], p[blocks // 2])
                y = jnp.concatenate([first, second], axis=1).astype(BF16)
                spec = jnp.dot(y, table[k], preferred_element_type=F32)
                filtered = (spec * gains[piece, j, :, pl.ds(k * 2 * LANES, 2 * LANES)]).astype(BF16)
                z = lax.dot_general(filtered, table[k], (((1,), (1,)), ((), ())), preferred_element_type=F32)
                pz[k] = z[:, :LANES]
                if k:
                    qz[k] = z[:, LANES:]
                else:
                    pz[blocks // 2] = z[:, LANES:]
            back = block_backward(pz, qz)
            early = []
            for owner in range(gy):
                parts = back[owner * nb : (owner + 1) * nb]
                tall = jnp.concatenate(parts, axis=0)
                if piece == last and j == 0:
                    tall = tall + landed[owner]
                bsend[piece, j, owner] = filled(tall, padded).astype(BF16)
                if piece == last:
                    ends = []
                    for row in (0, rows - 1):
                        ends.append(filled(
                            jnp.concatenate([tall[i * rows + row : i * rows + row + 1] for i in range(nb)], axis=0), 8
                        ))
                    esend[j, owner] = jnp.concatenate(ends, axis=0).astype(BF16)
            if piece == last:
                early = exchange(esend, erecv, esend_sem, erecv_sem, j)
            sent.append((exchange(bsend, brecv, bsend_sem, brecv_sem, piece, j), early))
        return sent

    def widened(tall, height):
        return jnp.concatenate([tall[i * height : (i + 1) * height] for i in range(nb)], axis=1)

    def send_halo(piece):
        low, high = pieces[piece]
        span = pl.ds(low, high - low)
        halo = []
        for way, side in ((0, left), (1, right)):
            copy = pltpu.make_async_remote_copy(
                src_ref=edges.at[way, span],
                dst_ref=halos.at[way, span],
                send_sem=hsend_sem.at[piece, way],
                recv_sem=hrecv_sem.at[piece, way],
                device_id={"gx": side},
                device_id_type=MESH,
            )
            copy.start()
            halo.append(copy)
        return halo

    def early_halo(piece, sent):
        low = pieces[piece][0]
        for j in counts(piece):
            for copy in sent[j][1].values():
                copy.wait_recv()
            for owner in range(gy):
                level = low + j * gy + owner
                ends = erecv[j, owner].astype(F32)
                for way, row in ((0, 0), (1, rows - 1)):
                    added = widened(ends[way * 8 : way * 8 + nb], 1)
                    edges[way, pl.ds(level, 1), :] = fields[level, pl.ds(row, 1), :] + added
        return send_halo(piece)

    def late_halo(piece, sent):
        low = pieces[piece][0]
        for j in counts(piece):
            for copy in sent[j][0].values():
                copy.wait_recv()
            for owner in range(gy):
                level = low + j * gy + owner
                updated = fields[level] + widened(brecv[piece, j, owner].astype(F32), rows)
                fields[level] = updated
                edges[0, pl.ds(level, 1), :] = updated[:1]
                edges[1, pl.ds(level, 1), :] = updated[rows - 1 :]
        return send_halo(piece)

    def finish_level(level, values, at):
        row = lax.broadcasted_iota(jnp.int32, (rows, cols), 0)
        keep = jnp.where(section == 1, land[...].astype(F32), 1.0)
        above = jnp.where(g == gx - 1, 0.0, 1.0)
        below = jnp.where(g == 0, 0.0, 1.0)
        after = jnp.where(row == rows - 1, halos[0, pl.ds(level, 1), :] * above, pltpu.roll(values, rows - 1, 0))
        before = jnp.where(row == 0, halos[1, pl.ds(level, 1), :] * below, pltpu.roll(values, 1, 0))
        outv[level] = (values + rate[...] * (after + before - 2.0 * values)) * keep
        write = pltpu.make_async_copy(outv.at[level], out_ref.at[level], out_sem.at[at])
        write.start()
        return write

    def cells(index):
        row = ((index.astype(F32) + 0.5) * np.float32(1.0 / cols)).astype(jnp.int32)
        return row, index - row * cols

    def gather_couplings():
        wide = 2 * LANES if cols % (2 * LANES) == 0 else LANES
        parts = cols // wide
        chunk = gy * slots
        surface = jnp.concatenate(
            [fields[c, :, pl.ds(i * wide, wide)] for c in range(FC) for i in range(parts)], axis=0
        ).astype(BF16)

        @pl.loop(0, gx)
        def _(way):
            base = way * gy
            index = jnp.concatenate([src_ref[pl.ds(base + i, 1), :] for i in range(gy)], axis=1)
            row, col = cells(index)
            part = col // wide
            pick = jnp.where(lax.broadcasted_iota(jnp.int32, (wide, chunk), 0) == col - part * wide, 1.0, 0.0)
            found = jnp.dot(surface, pick.astype(BF16), preferred_element_type=F32).reshape(FC, parts * rows, chunk)
            mine = (lax.broadcasted_iota(jnp.int32, (parts * rows, chunk), 0) == part * rows + row)[None]
            values = jnp.sum(jnp.where(mine, found, 0.0), axis=1)
            for i in range(gy):
                slot = lax.broadcasted_iota(jnp.int32, (1, slots), 1)
                weight = jnp.where(slot < count_ref[base + i], weight_ref[pl.ds(base + i, 1), :], 0.0)
                scaled = values[:, i * slots : (i + 1) * slots] * weight
                for c in range(FC):
                    sendc[way * FC + c, pl.ds(i, 1), :] = scaled[c : c + 1]

    def couple_copy(target):
        return pltpu.make_async_remote_copy(
            src_ref=sendc.at[target],
            dst_ref=recvc.at[me],
            send_sem=csend_sem,
            recv_sem=crecv_sem,
            device_id={"comp": 1 - section, "gx": target // FC, "gy": target % FC},
            device_id_type=MESH,
        )

    couplings = pltpu.make_async_remote_copy(
        src_ref=sendc, dst_ref=recvc, send_sem=csend_sem, recv_sem=crecv_sem,
        device_id={"comp": 1 - section}, device_id_type=MESH,
    )

    def land_couplings():
        couplings.wait_recv()
        per = CHUNK // slots
        for source in range(gy):
            def chunk_sum(c, total):
                base = c * per
                index = dsts[source, pl.ds(base, per), :]
                index = jnp.concatenate([index[i : i + 1] for i in range(per)], axis=1)
                values = jnp.concatenate([recvc[base + i, pl.ds(source, 1), :] for i in range(per)], axis=1)
                row, col = cells(index)
                block = col // LANES
                mine = lax.broadcasted_iota(jnp.int32, (lines, CHUNK), 0) == block * rows + row
                lane = lax.broadcasted_iota(jnp.int32, (LANES, CHUNK), 0) == col - block * LANES
                return total + lax.dot_general(
                    jnp.where(mine, 1.0, 0.0).astype(BF16),
                    jnp.where(lane, values, 0.0).astype(BF16),
                    (((1,), (1,)), ((), ())),
                    preferred_element_type=F32,
                )

            landed[source] = lax.fori_loop(
                0, peers // per, chunk_sum, jnp.zeros((lines, LANES), F32), unroll=min(8, peers // per)
            )

    load_high.wait()
    if last:
        pack_piece(0)
    load_low.wait()
    pack_piece(last)
    load_dst.wait()
    pl.semaphore_wait(barrier, gy - 1 + 2 + peers)

    forward = {}
    if last:
        forward[0] = send_forward(0)
    indices = []
    for mask in far_first(gy):
        copy = along_y(dst_ref, dsts.at[h], isend_sem.at[mask], irecv_sem.at[mask], mask)
        copy.start()
        indices.append(copy)
    dsts[h] = dst_ref[...]
    load_src.wait()
    load_weight.wait()
    load_count.wait()
    gather_couplings()

    @pl.loop(0, gx * FC)
    def _(target):
        couple_copy(target).start()

    forward[last] = send_forward(last)
    load_place.wait()
    load_resp.wait()
    expand_gains()
    load_table.wait()
    backward = {}
    if last:
        backward[0] = transform(0, forward[0])
    for copy in indices:
        copy.wait_recv()
    if FC == gy:
        land_couplings()
    else:
        pl.when(h < FC)(land_couplings)

        @pl.when(h >= FC)
        def _():
            landed[...] = jnp.zeros_like(landed)

    backward[last] = transform(last, forward[last])
    load_rate.wait()
    load_land.wait()
    writes = []
    if last:
        halo = late_halo(0, backward[0])
        ends = early_halo(last, backward[last])
        for copy in halo:
            copy.wait_recv()
        for level in range(*pieces[0]):
            writes.append(finish_level(level, fields[level], level))
    else:
        halo = []
        ends = early_halo(last, backward[last])
    for copy in ends:
        copy.wait_recv()
    low = pieces[last][0]
    for j in counts(last):
        for mask in [0, *reversed(far_first(gy))]:
            if mask:
                backward[last][j][0][mask].wait_recv()
            owner = flipped(h, mask, gy)
            level = low + j * gy + owner
            updated = fields[level] + widened(brecv[last, j, owner].astype(F32), rows)
            writes.append(finish_level(level, updated, low + j * gy + mask))
    couplings.wait_send()
    for copy in [*indices, *halo, *ends]:
        copy.wait_send()
    for piece in range(len(pieces)):
        for j in counts(piece):
            for group in (forward[piece][j], *backward[piece][j]):
                for copy in (group.values() if group else ()):
                    copy.wait_send()
    for write in writes:
        write.wait()


def local(state, response, diffusion, land_mask, couple_src, couple_dst, couple_weight, couple_count):
    levels, rows, cols = state.shape[1:]
    gx, gy = lax.axis_size("gx"), lax.axis_size("gy")
    peers, slots = couple_src.shape[3:]
    cols_all = cols * gy
    blocks = cols_all // LANES
    pieces = phases(levels, gy)
    per_piece = (pieces[0][1] - pieces[0][0]) // gy
    lines = cols // LANES * rows
    padded = -(-lines // 16) * 16
    tables = jnp.asarray(lane_tables(cols_all))
    places = jnp.asarray(spread_table(blocks))
    hbm = pl.BlockSpec(memory_space=pltpu.HBM)
    stay = lambda value: pltpu.with_memory_space_constraint(value, pltpu.HBM)
    message = (len(pieces), per_piece, gy, padded, LANES)
    ends = (per_piece, gy, 16, LANES)
    dma = pltpu.SemaphoreType.DMA
    out = pl.pallas_call(
        functools.partial(kernel, gx, gy),
        out_shape=jax.ShapeDtypeStruct((levels, rows, cols), F32),
        in_specs=[hbm] * 10,
        out_specs=pl.BlockSpec(memory_space=pl.ANY),
        scratch_shapes=[
            pltpu.VMEM((levels, rows, cols), F32),
            pltpu.VMEM((levels, rows, cols), F32),
            pltpu.VMEM(tables.shape, BF16),
            pltpu.VMEM(places.shape, BF16),
            pltpu.VMEM((levels, cols_all), F32),
            pltpu.VMEM((len(pieces), per_piece, 1, cols_all), F32),
            pltpu.VMEM((rows, cols), F32),
            pltpu.VMEM((rows, cols), jnp.int32),
            pltpu.VMEM((peers, slots), jnp.int32),
            pltpu.VMEM((peers, slots), jnp.int32),
            pltpu.VMEM((peers, slots), F32),
            pltpu.SMEM((peers,), jnp.int32),
            pltpu.VMEM((gx * FC, gy, slots), F32),
            pltpu.VMEM((peers, gy, slots), F32),
            pltpu.VMEM((gy, peers, slots), jnp.int32),
            pltpu.VMEM((gy, lines, LANES), F32),
            pltpu.VMEM(message, BF16),
            pltpu.VMEM(message, BF16),
            pltpu.VMEM(message, BF16),
            pltpu.VMEM(message, BF16),
            pltpu.VMEM(ends, BF16),
            pltpu.VMEM(ends, BF16),
            pltpu.VMEM((2, levels, cols), F32),
            pltpu.VMEM((2, levels, cols), F32),
            dma((11,)),
            dma((levels,)),
            dma,
            dma,
            dma((gy,)),
            dma((gy,)),
            dma(message[:3]),
            dma(message[:3]),
            dma(message[:3]),
            dma(message[:3]),
            dma(ends[:2]),
            dma(ends[:2]),
            dma((len(pieces), 2)),
            dma((len(pieces), 2)),
        ],
        compiler_params=pltpu.CompilerParams(
            collective_id=0, has_side_effects=True, vmem_limit_bytes=48 * 1024 * 1024
        ),
    )(
        *map(
            stay,
            (
                state[0],
                response[0],
                diffusion[0],
                land_mask,
                couple_src.reshape(peers, slots),
                couple_dst.reshape(peers, slots),
                couple_weight.reshape(peers, slots),
                couple_count.reshape(peers),
                tables,
                places,
            ),
        )
    )
    return out[None]


def solution(mesh):
    return jax.shard_map(
        local,
        mesh=mesh,
        in_specs=(
            P("comp", None, "gx", "gy"),
            P("comp", None, None),
            P("comp", "gx", "gy"),
            P("gx", "gy"),
            P("comp", "gx", "gy", None, None),
            P("comp", "gx", "gy", None, None),
            P("comp", "gx", "gy", None, None),
            P("comp", "gx", "gy", None),
        ),
        out_specs=P("comp", None, "gx", "gy"),
        check_vma=False,
    )
```

```python
import functools
import math

import jax
import jax.numpy as jnp
import ml_dtypes
import numpy as np
from jax import lax
from jax.experimental import pallas as pl
from jax.experimental.pallas import tpu as pltpu
from jax.sharding import PartitionSpec as P

FC = 4
LANES = 128
CHUNK = 256
CUT = 24
MESH = pl.DeviceIdType.MESH
F32 = jnp.float32
BF16 = jnp.bfloat16


def lane_tables(cols):
    blocks = cols // LANES
    lane = np.arange(LANES)[:, None]
    step = np.arange(LANES // 2)[None, :]
    tables = np.zeros((blocks // 2, 2 * LANES, 2 * LANES), np.float64)
    for k in range(blocks // 2):
        for place, residue in enumerate((k, blocks - k) if k else (0, blocks // 2)):
            angle = 2.0 * math.pi / cols * (lane * (blocks * step + residue) % cols)
            cos, sin = np.cos(angle), np.sin(angle)
            span = slice(place * LANES, (place + 1) * LANES)
            if k:
                sign = -1.0 if place else 1.0
                tables[k, :LANES, span] = np.concatenate([cos, sin], axis=1)
                tables[k, LANES:, span] = np.concatenate([-sin, cos], axis=1) * sign
            else:
                tables[k, span, span] = np.concatenate([cos, sin], axis=1)
    return tables.astype(ml_dtypes.bfloat16)


def pair_order(blocks):
    order = [0, blocks // 2]
    for k in range(1, blocks // 2):
        order += [k, blocks - k]
    return order


def spread_table(blocks):
    table = np.zeros((blocks * 16, blocks * LANES), np.float32)
    for place, residue in enumerate(pair_order(blocks)):
        for lane in range(LANES):
            table[blocks * (lane % 16) + residue, place * LANES + lane] = 1.0
    return table.astype(ml_dtypes.bfloat16)


def weighted(terms):
    total = None
    for coef, value in terms:
        if abs(coef) < 1e-12:
            continue
        if abs(abs(coef) - 1.0) < 1e-12:
            if total is None:
                total = value if coef > 0 else -value
            else:
                total = total + value if coef > 0 else total - value
        else:
            scaled = value * np.float32(coef)
            total = scaled if total is None else total + scaled
    return total


def block_forward(x):
    n = len(x)
    half, quarter = n // 2, n // 4
    cos = lambda a, k: math.cos(2.0 * math.pi * (a * k % n) / n)
    sin = lambda a, k: math.sin(2.0 * math.pi * (a * k % n) / n)
    even = {a: x[a] + x[n - a] for a in range(1, half)}
    odd = {a: x[a] - x[n - a] for a in range(1, half)}
    even[0], even[half] = x[0], x[half]
    ee = {a: even[a] + even[half - a] for a in range(quarter)}
    eo = {a: even[a] - even[half - a] for a in range(quarter)}
    ee[quarter] = even[quarter]
    oe = {a: odd[a] - odd[half - a] for a in range(1, quarter)}
    oo = {a: odd[a] + odd[half - a] for a in range(1, quarter)}
    oo[quarter] = odd[quarter]
    p, q = {}, {}
    for k in range(half + 1):
        p[k] = weighted([(cos(a, k), v) for a, v in (eo if k % 2 else ee).items()])
        if 0 < k < half:
            q[k] = weighted([(sin(a, k), v) for a, v in (oo if k % 2 else oe).items()])
    return p, q


def block_backward(p, q):
    half = max(p)
    n, quarter = 2 * half, half // 2
    cos = lambda a, k: math.cos(2.0 * math.pi * (a * k % n) / n)
    sin = lambda a, k: math.sin(2.0 * math.pi * (a * k % n) / n)
    u, v = {}, {}
    for a in range(quarter + 1):
        ue = weighted([(cos(a, k), p[k]) for k in range(0, half + 1, 2)])
        uo = weighted([(cos(a, k), p[k]) for k in range(1, half + 1, 2)])
        if a == quarter:
            u[a] = ue
        else:
            u[a], u[half - a] = ue + uo, ue - uo
        if a:
            vo = weighted([(sin(a, k), q[k]) for k in range(1, half, 2)])
            if a == quarter:
                v[a] = vo
            else:
                ve = weighted([(sin(a, k), q[k]) for k in range(2, half, 2)])
                v[a], v[half - a] = vo + ve, vo - ve
    x = [None] * n
    x[0], x[half] = u[0], u[half]
    for a in range(1, half):
        x[a], x[n - a] = u[a] + v[a], u[a] - v[a]
    return x


def flipped(index, mask, size):
    total, bit = 0, 1
    while bit < size:
        digit = (index // bit) % 2
        total = total + bit * (1 - digit if mask & bit else digit)
        bit *= 2
    return total


def far_first(size):
    return sorted(range(1, size), key=lambda mask: (mask < size // 2, mask))


def phases(levels, rows, groups_y):
    if FC % groups_y == 0 and (levels - FC) % groups_y == 0:
        cut = CUT if rows > CUT else rows
        pieces = [(FC, levels, 0, rows, 0), (0, FC, 0, cut, 1)]
        return pieces + ([(0, FC, cut, rows - cut, 1)] if cut < rows else [])
    return [(0, levels, 0, rows, 0)]


def owned_sets(levels, groups_y):
    sets = {}
    for low, high, _, _, which in phases(levels, 1, groups_y):
        sets[which] = (low, (high - low) // groups_y)
    return [sets[which] for which in sorted(sets)]


def kernel(
    gx, gy, pieces, state_hbm, resp_hbm, rate_hbm, land_hbm, src_hbm, dst_hbm, weight_hbm, count_hbm, table_hbm, place_hbm,
    out_ref,
    fields, table, place, resp, gains, rate, land, src_ref, dst_ref, weight_ref, count_ref,
    sendc, recvc, short, dsts, landing, landed, esend, erecv, edges, halos,
    load_sem, csend_sem, crecv_sem, isend_sem, irecv_sem, esend_sem, erecv_sem, hsend_sem, hrecv_sem,
    *buffers,
):
    fsend, frecv, bsend, brecv, fsend_sem, frecv_sem, bsend_sem, brecv_sem = (
        buffers[i * len(pieces) : (i + 1) * len(pieces)] for i in range(8)
    )
    levels, rows, cols = fields.shape
    peers, slots = src_ref.shape
    nb = cols // LANES
    lines = nb * rows
    blocks = nb * gy
    owned = owned_sets(levels, gy)
    coupled = [piece for piece in range(len(pieces)) if pieces[piece][0] == 0]
    plain = [piece for piece in range(len(pieces)) if pieces[piece][0] > 0]
    section = lax.axis_index("comp")
    g = lax.axis_index("gx")
    h = lax.axis_index("gy")
    me = g * gy + h
    sides = ((g + gx - 1) % gx, (g + 1) % gx)
    ends = (0, rows - 1)
    masks = far_first(gy)
    leaving = []

    def load(source, target, at):
        copy = pltpu.make_async_copy(source, target, load_sem.at[at])
        copy.start()
        return copy

    load_high = load(state_hbm.at[pl.ds(FC, levels - FC)], fields.at[pl.ds(FC, levels - FC)], 0)
    load_low = load(state_hbm.at[pl.ds(0, FC)], fields.at[pl.ds(0, FC)], 1)

    load_dst = load(dst_hbm, dst_ref, 5)

    barrier = pltpu.get_barrier_semaphore()

    def greet(**device):
        pl.semaphore_signal(barrier, inc=1, device_id=device, device_id_type=MESH)

    for mask in masks:
        greet(gy=flipped(h, mask, gy))

    @pl.loop(0, peers)
    def _(q):
        greet(comp=1 - section, gx=q // gy, gy=q % gy)

    for side in sides:
        for mask in [*masks, 0]:
            greet(gx=side, gy=flipped(h, mask, gy))

    load_src = load(src_hbm, src_ref, 2)
    load_weight = load(weight_hbm, weight_ref, 3)
    load_count = load(count_hbm, count_ref, 4)

    def filled(tall, count):
        if count > tall.shape[0]:
            tall = jnp.concatenate([tall, jnp.zeros((count - tall.shape[0], LANES), F32)], axis=0)
        return tall

    def remote(source, target, send_sem, recv_sem, **device):
        copy = pltpu.make_async_remote_copy(
            src_ref=source,
            dst_ref=target,
            send_sem=send_sem,
            recv_sem=recv_sem,
            device_id=device,
            device_id_type=MESH,
        )
        copy.start()
        leaving.append(copy)
        return copy

    def exchange(source, target, send_sem, recv_sem, j):
        copies = {}
        for mask in masks:
            other = flipped(h, mask, gy)
            copies[mask] = remote(
                source.at[j, other], target.at[j, h], send_sem.at[j, mask], recv_sem.at[j, mask], gy=other
            )
        target[j, h] = source[j, h]
        return copies

    def counts(piece):
        low, high = pieces[piece][:2]
        return range((high - low) // gy)

    def pack_piece(piece):
        low, _, first, count, _ = pieces[piece]
        for j in counts(piece):
            for owner in range(gy):
                values = fields[low + j * gy + owner, pl.ds(first, count), :]
                tall = jnp.concatenate([values[:, i * LANES : (i + 1) * LANES] for i in range(nb)], axis=0)
                fsend[piece][j, owner] = filled(tall, fsend[piece].shape[2]).astype(BF16)

    def send_forward(piece):
        return [exchange(fsend[piece], frecv[piece], fsend_sem[piece], frecv_sem[piece], j) for j in counts(piece)]

    def expand_gains():
        groups, width = LANES // 16, blocks * 16
        rows_all = []
        for low, many in owned:
            for j in range(many):
                line = resp[pl.ds(low + j * gy + h, 1), :] * np.float32(2.0 / (groups * width))
                rows_all.append(jnp.concatenate([line[:, i * width : (i + 1) * width] for i in range(groups)], axis=0))
        values = jnp.concatenate(rows_all, axis=0)
        count = values.shape[0]
        top = values.astype(BF16)
        rest = (values - top.astype(F32)).astype(BF16)
        both = jnp.concatenate([top, rest], axis=0)
        lane = lax.broadcasted_iota(jnp.int32, (groups, 2 * LANES), 1) % LANES
        mine = lane // 16 == lax.broadcasted_iota(jnp.int32, (groups, 2 * LANES), 0)
        for k in range(blocks // 2):
            span = pl.ds(k * 2 * LANES, 2 * LANES)
            wide = jnp.dot(both, place[:, span], preferred_element_type=F32)
            wide = wide[:count] + wide[count:]
            at = 0
            for which, (_, many) in enumerate(owned):
                for j in range(many):
                    mixed = jnp.where(mine, wide[at : at + groups], 0.0)
                    gains[which, j, :, span] = jnp.sum(mixed, axis=0, keepdims=True)
                    at += groups

    def transform(piece, arriving):
        _, _, first, count, which = pieces[piece]
        tallest = nb * count
        sent, early = [], []
        for j in counts(piece):
            for copy in arriving[j].values():
                copy.wait_recv()
            joins = piece in coupled and j == 0

            def coupling(source, i):
                return landed[source, pl.ds(i * rows + first, count), :]

            x = []
            for source in range(gy):
                tall = frecv[piece][j, source].astype(F32)[:tallest]
                for i in range(nb):
                    part = tall[i * count : (i + 1) * count]
                    x.append(part + coupling(source, i) if joins else part)
            p, q = block_forward(x)
            pz, qz = {}, {}
            for k in range(blocks // 2):
                one, two = (p[k], q[k]) if k else (p[0], p[blocks // 2])
                y = jnp.concatenate([one, two], axis=1).astype(BF16)
                spec = jnp.dot(y, table[k], preferred_element_type=F32)
                filtered = (spec * gains[which, j, :, pl.ds(k * 2 * LANES, 2 * LANES)]).astype(BF16)
                z = lax.dot_general(filtered, table[k], (((1,), (1,)), ((), ())), preferred_element_type=F32)
                pz[k] = z[:, :LANES]
                if k:
                    qz[k] = z[:, LANES:]
                else:
                    pz[blocks // 2] = z[:, LANES:]
            back = block_backward(pz, qz)
            if joins:
                back = [part + coupling(a // nb, a % nb) for a, part in enumerate(back)]
            for way, row in enumerate(ends):
                if first <= row < first + count:
                    for owner in range(gy):
                        parts = [part[row - first : row - first + 1] for part in back[owner * nb : (owner + 1) * nb]]
                        esend[which, way, j, owner] = jnp.concatenate(parts, axis=1)
                    for mask in [*masks, 0]:
                        other = flipped(h, mask, gy)
                        early.append(remote(
                            esend.at[which, way, j, other], erecv.at[which, way, j, h],
                            esend_sem.at[which, way, j, mask], erecv_sem.at[which, way, j, mask],
                            gx=sides[way], gy=other,
                        ))
            for owner in range(gy):
                tall = jnp.concatenate(back[owner * nb : (owner + 1) * nb], axis=0)
                bsend[piece][j, owner] = filled(tall, bsend[piece].shape[2]).astype(BF16)
            sent.append(exchange(bsend[piece], brecv[piece], bsend_sem[piece], brecv_sem[piece], j))
        return sent, early

    def updated(piece, j, owner):
        low, _, first, count, _ = pieces[piece]
        tall = brecv[piece][j, owner].astype(F32)
        wide = jnp.concatenate([tall[i * count : (i + 1) * count] for i in range(nb)], axis=1)
        return fields[low + j * gy + owner, pl.ds(first, count), :] + wide

    def send_raw_edges():
        for level in range(levels):
            for way, row in enumerate(ends):
                edges[way, pl.ds(level, 1), :] = fields[level, pl.ds(row, 1), :]
        return [
            remote(edges.at[way], halos.at[way], hsend_sem.at[way], hrecv_sem.at[way], gx=sides[way])
            for way in range(2)
        ]

    def finish_level(which, j, owner, values):
        level = owned[which][0] + j * gy + owner
        row = lax.broadcasted_iota(jnp.int32, (rows, cols), 0)
        keep = jnp.where(section == 1, land[...].astype(F32), 1.0)
        above = jnp.where(g == gx - 1, 0.0, 1.0)
        below = jnp.where(g == 0, 0.0, 1.0)
        after, before = halos[0, pl.ds(level, 1), :], halos[1, pl.ds(level, 1), :]
        after, before = after + erecv[which, 0, j, owner], before + erecv[which, 1, j, owner]
        after = jnp.where(row == rows - 1, after * above, pltpu.roll(values, rows - 1, 0))
        before = jnp.where(row == 0, before * below, pltpu.roll(values, 1, 0))
        out_ref[level] = (values + rate[...] * (after + before - 2.0 * values)) * keep

    def cells(index):
        row = ((index.astype(F32) + 0.5) * np.float32(1.0 / cols)).astype(jnp.int32)
        return row, index - row * cols

    def gather_couplings():
        wide = 2 * LANES if cols % (2 * LANES) == 0 else LANES
        parts = cols // wide
        chunk = gy * slots
        surface = jnp.concatenate(
            [fields[c, :, pl.ds(i * wide, wide)] for c in range(FC) for i in range(parts)], axis=0
        ).astype(BF16)

        @pl.loop(0, gx)
        def _(way):
            base = way * gy
            index = jnp.concatenate([src_ref[pl.ds(base + i, 1), :] for i in range(gy)], axis=1)
            row, col = cells(index)
            part = col // wide
            pick = jnp.where(lax.broadcasted_iota(jnp.int32, (wide, chunk), 0) == col - part * wide, 1.0, 0.0)
            found = jnp.dot(surface, pick.astype(BF16), preferred_element_type=F32).reshape(FC, parts * rows, chunk)
            mine = (lax.broadcasted_iota(jnp.int32, (parts * rows, chunk), 0) == part * rows + row)[None]
            values = jnp.sum(jnp.where(mine, found, 0.0), axis=1)
            for i in range(gy):
                slot = lax.broadcasted_iota(jnp.int32, (1, slots), 1)
                weight = jnp.where(slot < count_ref[base + i], weight_ref[pl.ds(base + i, 1), :], 0.0)
                scaled = values[:, i * slots : (i + 1) * slots] * weight
                for c in range(FC):
                    sendc[way * FC + c, pl.ds(i, 1), :] = scaled[c : c + 1]

    def couple_copy(target):
        return pltpu.make_async_remote_copy(
            src_ref=sendc.at[target],
            dst_ref=recvc.at[me],
            send_sem=csend_sem,
            recv_sem=crecv_sem,
            device_id={"comp": 1 - section, "gx": target // FC, "gy": target % FC},
            device_id_type=MESH,
        )

    couplings = pltpu.make_async_remote_copy(
        src_ref=sendc, dst_ref=recvc, send_sem=csend_sem, recv_sem=crecv_sem,
        device_id={"comp": 1 - section}, device_id_type=MESH,
    )

    def land_couplings():
        couplings.wait_recv()
        per = CHUNK // slots
        landing[...] = dsts[...].astype(jnp.int32)
        for source in range(gy):
            def chunk_sum(c, total):
                base = c * per
                index = jnp.concatenate([landing[source, pl.ds(base + i, 1), :] for i in range(per)], axis=1)
                values = jnp.concatenate([recvc[base + i, pl.ds(source, 1), :] for i in range(per)], axis=1)
                row, col = cells(index)
                block = col // LANES
                mine = lax.broadcasted_iota(jnp.int32, (lines, CHUNK), 0) == block * rows + row
                lane = lax.broadcasted_iota(jnp.int32, (LANES, CHUNK), 0) == col - block * LANES
                return total + lax.dot_general(
                    jnp.where(mine, 1.0, 0.0).astype(BF16),
                    jnp.where(lane, values, 0.0).astype(BF16),
                    (((1,), (1,)), ((), ())),
                    preferred_element_type=F32,
                )

            landed[source] = lax.fori_loop(
                0, peers // per, chunk_sum, jnp.zeros((lines, LANES), F32), unroll=min(8, peers // per)
            )

    forward, backward = {}, {}
    load_high.wait()
    for piece in plain:
        pack_piece(piece)
    load_low.wait()
    for load_one in (load_src, load_weight, load_count):
        load_one.wait()
    gather_couplings()
    for piece in coupled:
        pack_piece(piece)
    load_dst.wait()
    short[...] = dst_ref[...].astype(jnp.int16)
    pl.semaphore_wait(barrier, gy - 1 + peers + 2 * gy)
    indices = []
    for mask in masks:
        other = flipped(h, mask, gy)
        indices.append(remote(short, dsts.at[h], isend_sem.at[mask], irecv_sem.at[mask], gy=other))
    dsts[h] = short[...]

    @pl.loop(0, gx * FC)
    def _(target):
        couple_copy(target).start()

    for piece in plain:
        forward[piece] = send_forward(piece)
    for piece in coupled:
        forward[piece] = send_forward(piece)
    halo = send_raw_edges()
    load_place = load(place_hbm, place, 6)
    load_resp = load(resp_hbm, resp, 7)
    load_table = load(table_hbm, table, 8)
    load_rate = load(rate_hbm, rate, 9)
    load_land = load(land_hbm, land, 10)
    load_place.wait()
    load_resp.wait()
    expand_gains()
    load_table.wait()
    for piece in plain:
        backward[piece] = transform(piece, forward[piece])
    for copy in indices:
        copy.wait_recv()
    if FC == gy:
        land_couplings()
    else:
        pl.when(h < FC)(land_couplings)

        @pl.when(h >= FC)
        def _():
            landed[...] = jnp.zeros_like(landed)

    for piece in coupled:
        backward[piece] = transform(piece, forward[piece])
    load_rate.wait()
    load_land.wait()
    for copy in halo:
        copy.wait_recv()
    for which in range(len(owned)):
        group = [piece for piece in range(len(pieces)) if pieces[piece][4] == which]
        for piece in group:
            for copy in backward[piece][1]:
                copy.wait_recv()
        for j in counts(group[0]):
            for mask in [0, *reversed(masks)]:
                owner = flipped(h, mask, gy)
                for piece in group:
                    if mask:
                        backward[piece][0][j][mask].wait_recv()
                finish_level(which, j, owner, jnp.concatenate([updated(piece, j, owner) for piece in group], axis=0))
    couplings.wait_send()
    for copy in leaving:
        copy.wait_send()


def local(state, response, diffusion, land_mask, couple_src, couple_dst, couple_weight, couple_count):
    levels, rows, cols = state.shape[1:]
    gx, gy = lax.axis_size("gx"), lax.axis_size("gy")
    peers, slots = couple_src.shape[3:]
    cols_all = cols * gy
    nb, blocks = cols // LANES, cols_all // LANES
    lines = nb * rows
    pieces = phases(levels, rows, gy)
    owned = owned_sets(levels, gy)
    many = max(count for _, count in owned)
    tables = jnp.asarray(lane_tables(cols_all))
    places = jnp.asarray(spread_table(blocks))
    hbm = pl.BlockSpec(memory_space=pltpu.HBM)
    stay = lambda value: pltpu.with_memory_space_constraint(value, pltpu.HBM)
    dma = pltpu.SemaphoreType.DMA
    messages = [
        ((high - low) // gy, gy, -(-(nb * count) // 16) * 16, LANES) for low, high, _, count, _ in pieces
    ]
    out = pl.pallas_call(
        functools.partial(kernel, gx, gy, pieces),
        out_shape=jax.ShapeDtypeStruct((levels, rows, cols), F32),
        in_specs=[hbm] * 10,
        out_specs=pl.BlockSpec(memory_space=pltpu.VMEM),
        scratch_shapes=[
            pltpu.VMEM((levels, rows, cols), F32),
            pltpu.VMEM(tables.shape, BF16),
            pltpu.VMEM(places.shape, BF16),
            pltpu.VMEM((levels, cols_all), F32),
            pltpu.VMEM((len(owned), many, 1, cols_all), F32),
            pltpu.VMEM((rows, cols), F32),
            pltpu.VMEM((rows, cols), jnp.int32),
            pltpu.VMEM((peers, slots), jnp.int32),
            pltpu.VMEM((peers, slots), jnp.int32),
            pltpu.VMEM((peers, slots), F32),
            pltpu.SMEM((peers,), jnp.int32),
            pltpu.VMEM((gx * FC, gy, slots), F32),
            pltpu.VMEM((peers, gy, slots), F32),
            pltpu.VMEM((peers, slots), jnp.int16),
            pltpu.VMEM((gy, peers, slots), jnp.int16),
            pltpu.VMEM((gy, peers, slots), jnp.int32),
            pltpu.VMEM((gy, lines, LANES), F32),
            pltpu.VMEM((len(owned), 2, many, gy, 1, cols), F32),
            pltpu.VMEM((len(owned), 2, many, gy, 1, cols), F32),
            pltpu.VMEM((2, levels, cols), F32),
            pltpu.VMEM((2, levels, cols), F32),
            dma((11,)),
            dma,
            dma,
            dma((gy,)),
            dma((gy,)),
            dma((len(owned), 2, many, gy)),
            dma((len(owned), 2, many, gy)),
            dma((2,)),
            dma((2,)),
            *[pltpu.VMEM(message, BF16) for _ in range(4) for message in messages],
            *[dma(message[:2]) for _ in range(4) for message in messages],
        ],
        compiler_params=pltpu.CompilerParams(
            collective_id=0, has_side_effects=True, vmem_limit_bytes=48 * 1024 * 1024
        ),
    )(
        *map(
            stay,
            (
                state[0],
                response[0],
                diffusion[0],
                land_mask,
                couple_src.reshape(peers, slots),
                couple_dst.reshape(peers, slots),
                couple_weight.reshape(peers, slots),
                couple_count.reshape(peers),
                tables,
                places,
            ),
        )
    )
    return out[None]


def solution(mesh):
    return jax.shard_map(
        local,
        mesh=mesh,
        in_specs=(
            P("comp", None, "gx", "gy"),
            P("comp", None, None),
            P("comp", "gx", "gy"),
            P("gx", "gy"),
            P("comp", "gx", "gy", None, None),
            P("comp", "gx", "gy", None, None),
            P("comp", "gx", "gy", None, None),
            P("comp", "gx", "gy", None),
        ),
        out_specs=P("comp", None, "gx", "gy"),
        check_vma=False,
    )
```

```python
import functools
import math

import jax
import jax.numpy as jnp
import ml_dtypes
import numpy as np
from jax import lax
from jax.experimental import pallas as pl
from jax.experimental.pallas import tpu as pltpu
from jax.sharding import PartitionSpec as P

FC = 4
LANES = 128
CHUNK = 256
CUT = 24
MESH = pl.DeviceIdType.MESH
F32 = jnp.float32
BF16 = jnp.bfloat16


def lane_tables(cols):
    blocks = cols // LANES
    lane = np.arange(LANES)[:, None]
    step = np.arange(LANES // 2)[None, :]
    tables = np.zeros((blocks // 2, 2 * LANES, 2 * LANES), np.float64)
    for k in range(blocks // 2):
        for place, residue in enumerate((k, blocks - k) if k else (0, blocks // 2)):
            angle = 2.0 * math.pi / cols * (lane * (blocks * step + residue) % cols)
            cos, sin = np.cos(angle), np.sin(angle)
            span = slice(place * LANES, (place + 1) * LANES)
            if k:
                sign = -1.0 if place else 1.0
                tables[k, :LANES, span] = np.concatenate([cos, sin], axis=1)
                tables[k, LANES:, span] = np.concatenate([-sin, cos], axis=1) * sign
            else:
                tables[k, span, span] = np.concatenate([cos, sin], axis=1)
    return tables.astype(ml_dtypes.bfloat16)


def pair_order(blocks):
    order = [0, blocks // 2]
    for k in range(1, blocks // 2):
        order += [k, blocks - k]
    return order


def spread_table(blocks):
    table = np.zeros((blocks * 16, blocks * LANES), np.float32)
    for place, residue in enumerate(pair_order(blocks)):
        for lane in range(LANES):
            table[blocks * (lane % 16) + residue, place * LANES + lane] = 1.0
    return table.astype(ml_dtypes.bfloat16)


def weighted(terms):
    total = None
    for coef, value in terms:
        if abs(coef) < 1e-12:
            continue
        if abs(abs(coef) - 1.0) < 1e-12:
            if total is None:
                total = value if coef > 0 else -value
            else:
                total = total + value if coef > 0 else total - value
        else:
            scaled = value * np.float32(coef)
            total = scaled if total is None else total + scaled
    return total


def block_forward(x):
    n = len(x)
    half, quarter = n // 2, n // 4
    cos = lambda a, k: math.cos(2.0 * math.pi * (a * k % n) / n)
    sin = lambda a, k: math.sin(2.0 * math.pi * (a * k % n) / n)
    even = {a: x[a] + x[n - a] for a in range(1, half)}
    odd = {a: x[a] - x[n - a] for a in range(1, half)}
    even[0], even[half] = x[0], x[half]
    ee = {a: even[a] + even[half - a] for a in range(quarter)}
    eo = {a: even[a] - even[half - a] for a in range(quarter)}
    ee[quarter] = even[quarter]
    oe = {a: odd[a] - odd[half - a] for a in range(1, quarter)}
    oo = {a: odd[a] + odd[half - a] for a in range(1, quarter)}
    oo[quarter] = odd[quarter]
    p, q = {}, {}
    for k in range(half + 1):
        p[k] = weighted([(cos(a, k), v) for a, v in (eo if k % 2 else ee).items()])
        if 0 < k < half:
            q[k] = weighted([(sin(a, k), v) for a, v in (oo if k % 2 else oe).items()])
    return p, q


def block_backward(p, q):
    half = max(p)
    n, quarter = 2 * half, half // 2
    cos = lambda a, k: math.cos(2.0 * math.pi * (a * k % n) / n)
    sin = lambda a, k: math.sin(2.0 * math.pi * (a * k % n) / n)
    u, v = {}, {}
    for a in range(quarter + 1):
        ue = weighted([(cos(a, k), p[k]) for k in range(0, half + 1, 2)])
        uo = weighted([(cos(a, k), p[k]) for k in range(1, half + 1, 2)])
        if a == quarter:
            u[a] = ue
        else:
            u[a], u[half - a] = ue + uo, ue - uo
        if a:
            vo = weighted([(sin(a, k), q[k]) for k in range(1, half, 2)])
            if a == quarter:
                v[a] = vo
            else:
                ve = weighted([(sin(a, k), q[k]) for k in range(2, half, 2)])
                v[a], v[half - a] = vo + ve, vo - ve
    x = [None] * n
    x[0], x[half] = u[0], u[half]
    for a in range(1, half):
        x[a], x[n - a] = u[a] + v[a], u[a] - v[a]
    return x


def flipped(index, mask, size):
    total, bit = 0, 1
    while bit < size:
        digit = (index // bit) % 2
        total = total + bit * (1 - digit if mask & bit else digit)
        bit *= 2
    return total


def far_first(size):
    return sorted(range(1, size), key=lambda mask: (mask < size // 2, mask))


def phases(levels, rows, groups_y):
    if FC % groups_y == 0 and (levels - FC) % groups_y == 0:
        cut = CUT if rows > CUT else rows
        pieces = [(FC, levels, 0, rows, 0), (0, FC, 0, cut, 1)]
        return pieces + ([(0, FC, cut, rows - cut, 1)] if cut < rows else [])
    return [(0, levels, 0, rows, 0)]


def owned_sets(levels, groups_y):
    sets = {}
    for low, high, _, _, which in phases(levels, 1, groups_y):
        sets[which] = (low, (high - low) // groups_y)
    return [sets[which] for which in sorted(sets)]


def kernel(
    gx, gy, pieces, state_hbm, resp_hbm, rate_hbm, land_hbm, src_hbm, dst_hbm, weight_hbm, count_hbm, table_hbm, place_hbm,
    out_ref,
    fields, table, place, resp, gains, rate, land, src_ref, dst_ref, weight_ref, count_ref,
    sendc, recvc, short, dsts, landing, landed, esend, erecv, edges, halos,
    load_sem, csend_sem, crecv_sem, isend_sem, irecv_sem, esend_sem, erecv_sem, hsend_sem, hrecv_sem,
    *buffers,
):
    fsend, frecv, bsend, brecv, fsend_sem, frecv_sem, bsend_sem, brecv_sem = (
        buffers[i * len(pieces) : (i + 1) * len(pieces)] for i in range(8)
    )
    levels, rows, cols = fields.shape
    peers, slots = src_ref.shape
    nb = cols // LANES
    lines = nb * rows
    blocks = nb * gy
    owned = owned_sets(levels, gy)
    coupled = [piece for piece in range(len(pieces)) if pieces[piece][0] == 0]
    plain = [piece for piece in range(len(pieces)) if pieces[piece][0] > 0]
    section = lax.axis_index("comp")
    g = lax.axis_index("gx")
    h = lax.axis_index("gy")
    me = g * gy + h
    sides = ((g + gx - 1) % gx, (g + 1) % gx)
    ends = (0, rows - 1)
    masks = far_first(gy)
    leaving = []

    def load(source, target, at):
        copy = pltpu.make_async_copy(source, target, load_sem.at[at])
        copy.start()
        return copy

    load_high = load(state_hbm.at[pl.ds(FC, levels - FC)], fields.at[pl.ds(FC, levels - FC)], 0)
    load_low = load(state_hbm.at[pl.ds(0, FC)], fields.at[pl.ds(0, FC)], 1)

    load_dst = load(dst_hbm, dst_ref, 5)

    barrier = pltpu.get_barrier_semaphore()

    def greet(**device):
        pl.semaphore_signal(barrier, inc=1, device_id=device, device_id_type=MESH)

    for mask in masks:
        greet(gy=flipped(h, mask, gy))

    @pl.loop(0, peers)
    def _(q):
        greet(comp=1 - section, gx=q // gy, gy=q % gy)

    for side in sides:
        for mask in [*masks, 0]:
            greet(gx=side, gy=flipped(h, mask, gy))

    load_src = load(src_hbm, src_ref, 2)
    load_weight = load(weight_hbm, weight_ref, 3)
    load_count = load(count_hbm, count_ref, 4)

    def filled(tall, count):
        if count > tall.shape[0]:
            tall = jnp.concatenate([tall, jnp.zeros((count - tall.shape[0], LANES), F32)], axis=0)
        return tall

    def remote(source, target, send_sem, recv_sem, **device):
        copy = pltpu.make_async_remote_copy(
            src_ref=source,
            dst_ref=target,
            send_sem=send_sem,
            recv_sem=recv_sem,
            device_id=device,
            device_id_type=MESH,
        )
        copy.start()
        leaving.append(copy)
        return copy

    def exchange(source, target, send_sem, recv_sem, j):
        copies = {}
        for mask in masks:
            other = flipped(h, mask, gy)
            copies[mask] = remote(
                source.at[j, other], target.at[j, h], send_sem.at[j, mask], recv_sem.at[j, mask], gy=other
            )
        target[j, h] = source[j, h]
        return copies

    def counts(piece):
        low, high = pieces[piece][:2]
        return range((high - low) // gy)

    def pack_piece(piece):
        low, _, first, count, _ = pieces[piece]
        for j in counts(piece):
            for owner in range(gy):
                values = fields[low + j * gy + owner, pl.ds(first, count), :]
                tall = jnp.concatenate([values[:, i * LANES : (i + 1) * LANES] for i in range(nb)], axis=0)
                fsend[piece][j, owner] = filled(tall, fsend[piece].shape[2]).astype(BF16)

    def send_forward(piece):
        return [exchange(fsend[piece], frecv[piece], fsend_sem[piece], frecv_sem[piece], j) for j in counts(piece)]

    def expand_gains():
        groups, width = LANES // 16, blocks * 16
        rows_all = []
        for low, many in owned:
            for j in range(many):
                line = resp[pl.ds(low + j * gy + h, 1), :] * np.float32(2.0 / (groups * width))
                rows_all.append(jnp.concatenate([line[:, i * width : (i + 1) * width] for i in range(groups)], axis=0))
        values = jnp.concatenate(rows_all, axis=0)
        count = values.shape[0]
        top = values.astype(BF16)
        rest = (values - top.astype(F32)).astype(BF16)
        both = jnp.concatenate([top, rest], axis=0)
        lane = lax.broadcasted_iota(jnp.int32, (groups, 2 * LANES), 1) % LANES
        mine = lane // 16 == lax.broadcasted_iota(jnp.int32, (groups, 2 * LANES), 0)
        for k in range(blocks // 2):
            span = pl.ds(k * 2 * LANES, 2 * LANES)
            wide = jnp.dot(both, place[:, span], preferred_element_type=F32)
            wide = wide[:count] + wide[count:]
            at = 0
            for which, (_, many) in enumerate(owned):
                for j in range(many):
                    mixed = jnp.where(mine, wide[at : at + groups], 0.0)
                    gains[which, j, :, span] = jnp.sum(mixed, axis=0, keepdims=True)
                    at += groups

    def transform(piece, arriving):
        _, _, first, count, which = pieces[piece]
        tallest = nb * count
        sent, early = [], []
        for j in counts(piece):
            for copy in arriving[j].values():
                copy.wait_recv()
            joins = piece in coupled and j == 0

            def coupling(source, i):
                return landed[source, pl.ds(i * rows + first, count), :]

            x = []
            for source in range(gy):
                tall = frecv[piece][j, source].astype(F32)[:tallest]
                for i in range(nb):
                    part = tall[i * count : (i + 1) * count]
                    x.append(part + coupling(source, i) if joins else part)
            p, q = block_forward(x)
            pz, qz = {}, {}
            for k in range(blocks // 2):
                one, two = (p[k], q[k]) if k else (p[0], p[blocks // 2])
                y = jnp.concatenate([one, two], axis=1).astype(BF16)
                spec = jnp.dot(y, table[k], preferred_element_type=F32)
                filtered = (spec * gains[which, j, :, pl.ds(k * 2 * LANES, 2 * LANES)]).astype(BF16)
                z = lax.dot_general(filtered, table[k], (((1,), (1,)), ((), ())), preferred_element_type=F32)
                pz[k] = z[:, :LANES]
                if k:
                    qz[k] = z[:, LANES:]
                else:
                    pz[blocks // 2] = z[:, LANES:]
            back = block_backward(pz, qz)
            if joins:
                back = [part + coupling(a // nb, a % nb) for a, part in enumerate(back)]
            for way, row in enumerate(ends):
                if first <= row < first + count:
                    for owner in range(gy):
                        parts = [part[row - first : row - first + 1] for part in back[owner * nb : (owner + 1) * nb]]
                        esend[which, way, j, owner] = jnp.concatenate(parts, axis=1)
                    for mask in [*masks, 0]:
                        other = flipped(h, mask, gy)
                        early.append(remote(
                            esend.at[which, way, j, other], erecv.at[which, way, j, h],
                            esend_sem.at[which, way, j, mask], erecv_sem.at[which, way, j, mask],
                            gx=sides[way], gy=other,
                        ))
            for owner in range(gy):
                tall = jnp.concatenate(back[owner * nb : (owner + 1) * nb], axis=0)
                bsend[piece][j, owner] = filled(tall, bsend[piece].shape[2]).astype(BF16)
            sent.append(exchange(bsend[piece], brecv[piece], bsend_sem[piece], brecv_sem[piece], j))
        return sent, early

    def updated(piece, j, owner):
        low, _, first, count, _ = pieces[piece]
        tall = brecv[piece][j, owner].astype(F32)
        wide = jnp.concatenate([tall[i * count : (i + 1) * count] for i in range(nb)], axis=1)
        return fields[low + j * gy + owner, pl.ds(first, count), :] + wide

    def send_raw_edges():
        for level in range(levels):
            for way, row in enumerate(ends):
                edges[way, pl.ds(level, 1), :] = fields[level, pl.ds(row, 1), :]
        return [
            remote(edges.at[way], halos.at[way], hsend_sem.at[way], hrecv_sem.at[way], gx=sides[way])
            for way in range(2)
        ]

    def finish_level(which, j, owner, values):
        level = owned[which][0] + j * gy + owner
        row = lax.broadcasted_iota(jnp.int32, (rows, cols), 0)
        keep = jnp.where(section == 1, land[...].astype(F32), 1.0)
        above = jnp.where(g == gx - 1, 0.0, 1.0)
        below = jnp.where(g == 0, 0.0, 1.0)
        after, before = halos[0, pl.ds(level, 1), :], halos[1, pl.ds(level, 1), :]
        after, before = after + erecv[which, 0, j, owner], before + erecv[which, 1, j, owner]
        after = jnp.where(row == rows - 1, after * above, pltpu.roll(values, rows - 1, 0))
        before = jnp.where(row == 0, before * below, pltpu.roll(values, 1, 0))
        out_ref[level] = (values + rate[...] * (after + before - 2.0 * values)) * keep

    def cells(index):
        row = ((index.astype(F32) + 0.5) * np.float32(1.0 / cols)).astype(jnp.int32)
        return row, index - row * cols

    def gather_couplings():
        wide = 2 * LANES if cols % (2 * LANES) == 0 else LANES
        parts = cols // wide
        chunk = gy * slots
        surface = jnp.concatenate(
            [fields[c, :, pl.ds(i * wide, wide)] for c in range(FC) for i in range(parts)], axis=0
        ).astype(BF16)

        @pl.loop(0, gx)
        def _(way):
            base = way * gy
            index = jnp.concatenate([src_ref[pl.ds(base + i, 1), :] for i in range(gy)], axis=1)
            row, col = cells(index)
            part = col // wide
            pick = jnp.where(lax.broadcasted_iota(jnp.int32, (wide, chunk), 0) == col - part * wide, 1.0, 0.0)
            found = jnp.dot(surface, pick.astype(BF16), preferred_element_type=F32).reshape(FC, parts * rows, chunk)
            mine = (lax.broadcasted_iota(jnp.int32, (parts * rows, chunk), 0) == part * rows + row)[None]
            values = jnp.sum(jnp.where(mine, found, 0.0), axis=1)
            scaled = []
            for i in range(gy):
                slot = lax.broadcasted_iota(jnp.int32, (1, slots), 1)
                weight = jnp.where(slot < count_ref[base + i], weight_ref[pl.ds(base + i, 1), :], 0.0)
                scaled.append(values[:, i * slots : (i + 1) * slots] * weight)
            for c in range(FC):
                sendc[way * FC + c] = jnp.concatenate([part[c : c + 1] for part in scaled], axis=0).astype(BF16)

    def couple_copy(target):
        return pltpu.make_async_remote_copy(
            src_ref=sendc.at[target],
            dst_ref=recvc.at[me],
            send_sem=csend_sem,
            recv_sem=crecv_sem,
            device_id={"comp": 1 - section, "gx": target // FC, "gy": target % FC},
            device_id_type=MESH,
        )

    couplings = pltpu.make_async_remote_copy(
        src_ref=sendc, dst_ref=recvc, send_sem=csend_sem, recv_sem=crecv_sem,
        device_id={"comp": 1 - section}, device_id_type=MESH,
    )

    def land_couplings():
        couplings.wait_recv()
        per = CHUNK // slots
        landing[...] = dsts[...].astype(jnp.int32)
        for source in range(gy):
            def chunk_sum(c, total):
                base = c * per
                index = jnp.concatenate([landing[source, pl.ds(base + i, 1), :] for i in range(per)], axis=1)
                values = [recvc[base + i].astype(F32)[source : source + 1] for i in range(per)]
                values = jnp.concatenate(values, axis=1)
                row, col = cells(index)
                block = col // LANES
                mine = lax.broadcasted_iota(jnp.int32, (lines, CHUNK), 0) == block * rows + row
                lane = lax.broadcasted_iota(jnp.int32, (LANES, CHUNK), 0) == col - block * LANES
                return total + lax.dot_general(
                    jnp.where(mine, 1.0, 0.0).astype(BF16),
                    jnp.where(lane, values, 0.0).astype(BF16),
                    (((1,), (1,)), ((), ())),
                    preferred_element_type=F32,
                )

            landed[source] = lax.fori_loop(
                0, peers // per, chunk_sum, jnp.zeros((lines, LANES), F32), unroll=min(8, peers // per)
            )

    forward, backward = {}, {}
    load_high.wait()
    for piece in plain:
        pack_piece(piece)
    load_low.wait()
    for load_one in (load_src, load_weight, load_count):
        load_one.wait()
    gather_couplings()
    for piece in coupled:
        pack_piece(piece)
    load_dst.wait()
    short[...] = dst_ref[...].astype(jnp.int16)
    pl.semaphore_wait(barrier, gy - 1 + peers + 2 * gy)
    indices = []
    for mask in masks:
        other = flipped(h, mask, gy)
        indices.append(remote(short, dsts.at[h], isend_sem.at[mask], irecv_sem.at[mask], gy=other))
    dsts[h] = short[...]

    @pl.loop(0, gx * FC)
    def _(target):
        couple_copy(target).start()

    for piece in plain:
        forward[piece] = send_forward(piece)
    for piece in coupled:
        forward[piece] = send_forward(piece)
    halo = send_raw_edges()
    load_place = load(place_hbm, place, 6)
    load_resp = load(resp_hbm, resp, 7)
    load_table = load(table_hbm, table, 8)
    load_rate = load(rate_hbm, rate, 9)
    load_land = load(land_hbm, land, 10)
    load_place.wait()
    load_resp.wait()
    expand_gains()
    load_table.wait()
    for piece in plain:
        backward[piece] = transform(piece, forward[piece])
    for copy in indices:
        copy.wait_recv()
    if FC == gy:
        land_couplings()
    else:
        pl.when(h < FC)(land_couplings)

        @pl.when(h >= FC)
        def _():
            landed[...] = jnp.zeros_like(landed)

    for piece in coupled:
        backward[piece] = transform(piece, forward[piece])
    load_rate.wait()
    load_land.wait()
    for copy in halo:
        copy.wait_recv()
    for which in range(len(owned)):
        group = [piece for piece in range(len(pieces)) if pieces[piece][4] == which]
        for piece in group:
            for copy in backward[piece][1]:
                copy.wait_recv()
        for j in counts(group[0]):
            for mask in [0, *reversed(masks)]:
                owner = flipped(h, mask, gy)
                for piece in group:
                    if mask:
                        backward[piece][0][j][mask].wait_recv()
                finish_level(which, j, owner, jnp.concatenate([updated(piece, j, owner) for piece in group], axis=0))
    couplings.wait_send()
    for copy in leaving:
        copy.wait_send()


def local(state, response, diffusion, land_mask, couple_src, couple_dst, couple_weight, couple_count):
    levels, rows, cols = state.shape[1:]
    gx, gy = lax.axis_size("gx"), lax.axis_size("gy")
    peers, slots = couple_src.shape[3:]
    cols_all = cols * gy
    nb, blocks = cols // LANES, cols_all // LANES
    lines = nb * rows
    pieces = phases(levels, rows, gy)
    owned = owned_sets(levels, gy)
    many = max(count for _, count in owned)
    tables = jnp.asarray(lane_tables(cols_all))
    places = jnp.asarray(spread_table(blocks))
    hbm = pl.BlockSpec(memory_space=pltpu.HBM)
    stay = lambda value: pltpu.with_memory_space_constraint(value, pltpu.HBM)
    dma = pltpu.SemaphoreType.DMA
    messages = [
        ((high - low) // gy, gy, -(-(nb * count) // 16) * 16, LANES) for low, high, _, count, _ in pieces
    ]
    out = pl.pallas_call(
        functools.partial(kernel, gx, gy, pieces),
        out_shape=jax.ShapeDtypeStruct((levels, rows, cols), F32),
        in_specs=[hbm] * 10,
        out_specs=pl.BlockSpec(memory_space=pltpu.VMEM),
        scratch_shapes=[
            pltpu.VMEM((levels, rows, cols), F32),
            pltpu.VMEM(tables.shape, BF16),
            pltpu.VMEM(places.shape, BF16),
            pltpu.VMEM((levels, cols_all), F32),
            pltpu.VMEM((len(owned), many, 1, cols_all), F32),
            pltpu.VMEM((rows, cols), F32),
            pltpu.VMEM((rows, cols), jnp.int32),
            pltpu.VMEM((peers, slots), jnp.int32),
            pltpu.VMEM((peers, slots), jnp.int32),
            pltpu.VMEM((peers, slots), F32),
            pltpu.SMEM((peers,), jnp.int32),
            pltpu.VMEM((gx * FC, gy, slots), BF16),
            pltpu.VMEM((peers, gy, slots), BF16),
            pltpu.VMEM((peers, slots), jnp.int16),
            pltpu.VMEM((gy, peers, slots), jnp.int16),
            pltpu.VMEM((gy, peers, slots), jnp.int32),
            pltpu.VMEM((gy, lines, LANES), F32),
            pltpu.VMEM((len(owned), 2, many, gy, 1, cols), F32),
            pltpu.VMEM((len(owned), 2, many, gy, 1, cols), F32),
            pltpu.VMEM((2, levels, cols), F32),
            pltpu.VMEM((2, levels, cols), F32),
            dma((11,)),
            dma,
            dma,
            dma((gy,)),
            dma((gy,)),
            dma((len(owned), 2, many, gy)),
            dma((len(owned), 2, many, gy)),
            dma((2,)),
            dma((2,)),
            *[pltpu.VMEM(message, BF16) for _ in range(4) for message in messages],
            *[dma(message[:2]) for _ in range(4) for message in messages],
        ],
        compiler_params=pltpu.CompilerParams(
            collective_id=0, has_side_effects=True, vmem_limit_bytes=48 * 1024 * 1024
        ),
    )(
        *map(
            stay,
            (
                state[0],
                response[0],
                diffusion[0],
                land_mask,
                couple_src.reshape(peers, slots),
                couple_dst.reshape(peers, slots),
                couple_weight.reshape(peers, slots),
                couple_count.reshape(peers),
                tables,
                places,
            ),
        )
    )
    return out[None]


def solution(mesh):
    return jax.shard_map(
        local,
        mesh=mesh,
        in_specs=(
            P("comp", None, "gx", "gy"),
            P("comp", None, None),
            P("comp", "gx", "gy"),
            P("gx", "gy"),
            P("comp", "gx", "gy", None, None),
            P("comp", "gx", "gy", None, None),
            P("comp", "gx", "gy", None, None),
            P("comp", "gx", "gy", None),
        ),
        out_specs=P("comp", None, "gx", "gy"),
        check_vma=False,
    )
```

```python
import functools
import math

import jax
import jax.numpy as jnp
import ml_dtypes
import numpy as np
from jax import lax
from jax.experimental import pallas as pl
from jax.experimental.pallas import tpu as pltpu
from jax.sharding import PartitionSpec as P

FC = 4
LANES = 128
CHUNK = 256
CUT = 24
MESH = pl.DeviceIdType.MESH
F32 = jnp.float32
BF16 = jnp.bfloat16


def lane_tables(cols):
    blocks = cols // LANES
    lane = np.arange(LANES)[:, None]
    step = np.arange(LANES // 2)[None, :]
    tables = np.zeros((blocks // 2, 2 * LANES, 2 * LANES), np.float64)
    for k in range(blocks // 2):
        for place, residue in enumerate((k, blocks - k) if k else (0, blocks // 2)):
            angle = 2.0 * math.pi / cols * (lane * (blocks * step + residue) % cols)
            cos, sin = np.cos(angle), np.sin(angle)
            span = slice(place * LANES, (place + 1) * LANES)
            if k:
                sign = -1.0 if place else 1.0
                tables[k, :LANES, span] = np.concatenate([cos, sin], axis=1)
                tables[k, LANES:, span] = np.concatenate([-sin, cos], axis=1) * sign
            else:
                tables[k, span, span] = np.concatenate([cos, sin], axis=1)
    return tables.astype(ml_dtypes.bfloat16)


def pair_order(blocks):
    order = [0, blocks // 2]
    for k in range(1, blocks // 2):
        order += [k, blocks - k]
    return order


def spread_table(blocks):
    table = np.zeros((blocks * 16, blocks * LANES), np.float32)
    for place, residue in enumerate(pair_order(blocks)):
        for lane in range(LANES):
            table[blocks * (lane % 16) + residue, place * LANES + lane] = 1.0
    return table.astype(ml_dtypes.bfloat16)


def weighted(terms):
    total = None
    for coef, value in terms:
        if abs(coef) < 1e-12:
            continue
        if abs(abs(coef) - 1.0) < 1e-12:
            if total is None:
                total = value if coef > 0 else -value
            else:
                total = total + value if coef > 0 else total - value
        else:
            scaled = value * np.float32(coef)
            total = scaled if total is None else total + scaled
    return total


def block_forward(x):
    n = len(x)
    half, quarter = n // 2, n // 4
    cos = lambda a, k: math.cos(2.0 * math.pi * (a * k % n) / n)
    sin = lambda a, k: math.sin(2.0 * math.pi * (a * k % n) / n)
    even = {a: x[a] + x[n - a] for a in range(1, half)}
    odd = {a: x[a] - x[n - a] for a in range(1, half)}
    even[0], even[half] = x[0], x[half]
    ee = {a: even[a] + even[half - a] for a in range(quarter)}
    eo = {a: even[a] - even[half - a] for a in range(quarter)}
    ee[quarter] = even[quarter]
    oe = {a: odd[a] - odd[half - a] for a in range(1, quarter)}
    oo = {a: odd[a] + odd[half - a] for a in range(1, quarter)}
    oo[quarter] = odd[quarter]
    p, q = {}, {}
    for k in range(half + 1):
        p[k] = weighted([(cos(a, k), v) for a, v in (eo if k % 2 else ee).items()])
        if 0 < k < half:
            q[k] = weighted([(sin(a, k), v) for a, v in (oo if k % 2 else oe).items()])
    return p, q


def block_backward(p, q):
    half = max(p)
    n, quarter = 2 * half, half // 2
    cos = lambda a, k: math.cos(2.0 * math.pi * (a * k % n) / n)
    sin = lambda a, k: math.sin(2.0 * math.pi * (a * k % n) / n)
    u, v = {}, {}
    for a in range(quarter + 1):
        ue = weighted([(cos(a, k), p[k]) for k in range(0, half + 1, 2)])
        uo = weighted([(cos(a, k), p[k]) for k in range(1, half + 1, 2)])
        if a == quarter:
            u[a] = ue
        else:
            u[a], u[half - a] = ue + uo, ue - uo
        if a:
            vo = weighted([(sin(a, k), q[k]) for k in range(1, half, 2)])
            if a == quarter:
                v[a] = vo
            else:
                ve = weighted([(sin(a, k), q[k]) for k in range(2, half, 2)])
                v[a], v[half - a] = vo + ve, vo - ve
    x = [None] * n
    x[0], x[half] = u[0], u[half]
    for a in range(1, half):
        x[a], x[n - a] = u[a] + v[a], u[a] - v[a]
    return x


def flipped(index, mask, size):
    total, bit = 0, 1
    while bit < size:
        digit = (index // bit) % 2
        total = total + bit * (1 - digit if mask & bit else digit)
        bit *= 2
    return total


def far_first(size):
    return sorted(range(1, size), key=lambda mask: (mask < size // 2, mask))


def phases(levels, rows, groups_y):
    if FC % groups_y == 0 and (levels - FC) % groups_y == 0:
        cut = CUT if rows > CUT else rows
        pieces = [(FC, levels, 0, rows, 0), (0, FC, 0, cut, 1)]
        return pieces + ([(0, FC, cut, rows - cut, 1)] if cut < rows else [])
    return [(0, levels, 0, rows, 0)]


def owned_sets(levels, groups_y):
    sets = {}
    for low, high, _, _, which in phases(levels, 1, groups_y):
        sets[which] = (low, (high - low) // groups_y)
    return [sets[which] for which in sorted(sets)]


def kernel(
    gx, gy, pieces, state_hbm, resp_hbm, rate_hbm, land_hbm, src_hbm, dst_hbm, weight_hbm, count_hbm, table_hbm, place_hbm,
    out_ref,
    fields, table, place, resp, gains, rate, land, src_ref, dst_ref, weight_ref, count_ref,
    sendc, recvc, short, dsts, landing, landed, esend, erecv, edges, halos,
    load_sem, csend_sem, crecv_sem, isend_sem, irecv_sem, esend_sem, erecv_sem, hsend_sem, hrecv_sem,
    *buffers,
):
    fsend, frecv, bsend, brecv, fsend_sem, frecv_sem, bsend_sem, brecv_sem = (
        buffers[i * len(pieces) : (i + 1) * len(pieces)] for i in range(8)
    )
    levels, rows, cols = fields.shape
    peers, slots = src_ref.shape
    nb = cols // LANES
    lines = nb * rows
    blocks = nb * gy
    owned = owned_sets(levels, gy)
    coupled = [piece for piece in range(len(pieces)) if pieces[piece][0] == 0]
    plain = [piece for piece in range(len(pieces)) if pieces[piece][0] > 0]
    section = lax.axis_index("comp")
    g = lax.axis_index("gx")
    h = lax.axis_index("gy")
    me = g * gy + h
    sides = ((g + gx - 1) % gx, (g + 1) % gx)
    ends = (0, rows - 1)
    masks = far_first(gy)
    leaving = []

    def load(source, target, at):
        copy = pltpu.make_async_copy(source, target, load_sem.at[at])
        copy.start()
        return copy

    load_high = load(state_hbm.at[pl.ds(FC, levels - FC)], fields.at[pl.ds(FC, levels - FC)], 0)
    load_low = load(state_hbm.at[pl.ds(0, FC)], fields.at[pl.ds(0, FC)], 1)

    load_dst = load(dst_hbm, dst_ref, 5)

    barrier = pltpu.get_barrier_semaphore()

    def greet(**device):
        pl.semaphore_signal(barrier, inc=1, device_id=device, device_id_type=MESH)

    for mask in masks:
        greet(gy=flipped(h, mask, gy))

    @pl.loop(0, peers)
    def _(q):
        greet(comp=1 - section, gx=q // gy, gy=q % gy)

    for side in sides:
        for mask in [*masks, 0]:
            greet(gx=side, gy=flipped(h, mask, gy))

    load_src = load(src_hbm, src_ref, 2)
    load_weight = load(weight_hbm, weight_ref, 3)
    load_count = load(count_hbm, count_ref, 4)

    def filled(tall, count):
        if count > tall.shape[0]:
            tall = jnp.concatenate([tall, jnp.zeros((count - tall.shape[0], LANES), F32)], axis=0)
        return tall

    def remote(source, target, send_sem, recv_sem, **device):
        copy = pltpu.make_async_remote_copy(
            src_ref=source,
            dst_ref=target,
            send_sem=send_sem,
            recv_sem=recv_sem,
            device_id=device,
            device_id_type=MESH,
        )
        copy.start()
        leaving.append(copy)
        return copy

    def exchange(source, target, send_sem, recv_sem, j):
        copies = {}
        for mask in masks:
            other = flipped(h, mask, gy)
            copies[mask] = remote(
                source.at[j, other], target.at[j, h], send_sem.at[j, mask], recv_sem.at[j, mask], gy=other
            )
        target[j, h] = source[j, h]
        return copies

    def counts(piece):
        low, high = pieces[piece][:2]
        return range((high - low) // gy)

    def pack_piece(piece):
        low, _, first, count, _ = pieces[piece]
        for j in counts(piece):
            for owner in range(gy):
                values = fields[low + j * gy + owner, pl.ds(first, count), :]
                tall = jnp.concatenate([values[:, i * LANES : (i + 1) * LANES] for i in range(nb)], axis=0)
                fsend[piece][j, owner] = filled(tall, fsend[piece].shape[2]).astype(BF16)

    def send_forward(piece):
        return [exchange(fsend[piece], frecv[piece], fsend_sem[piece], frecv_sem[piece], j) for j in counts(piece)]

    def expand_gains():
        groups, width = LANES // 16, blocks * 16
        rows_all = []
        for low, many in owned:
            for j in range(many):
                line = resp[pl.ds(low + j * gy + h, 1), :] * np.float32(2.0 / (groups * width))
                rows_all.append(jnp.concatenate([line[:, i * width : (i + 1) * width] for i in range(groups)], axis=0))
        values = jnp.concatenate(rows_all, axis=0)
        count = values.shape[0]
        top = values.astype(BF16)
        rest = (values - top.astype(F32)).astype(BF16)
        both = jnp.concatenate([top, rest], axis=0)
        lane = lax.broadcasted_iota(jnp.int32, (groups, 2 * LANES), 1) % LANES
        mine = lane // 16 == lax.broadcasted_iota(jnp.int32, (groups, 2 * LANES), 0)
        for k in range(blocks // 2):
            span = pl.ds(k * 2 * LANES, 2 * LANES)
            wide = jnp.dot(both, place[:, span], preferred_element_type=F32)
            wide = wide[:count] + wide[count:]
            at = 0
            for which, (_, many) in enumerate(owned):
                for j in range(many):
                    mixed = jnp.where(mine, wide[at : at + groups], 0.0)
                    gains[which, j, :, span] = jnp.sum(mixed, axis=0, keepdims=True)
                    at += groups

    def transform(piece, arriving):
        _, _, first, count, which = pieces[piece]
        tallest = nb * count
        sent, early = [], []
        for j in counts(piece):
            for copy in arriving[j].values():
                copy.wait_recv()
            joins = piece in coupled and j == 0

            def coupling(source, i):
                return landed[source, pl.ds(i * rows + first, count), :]

            x = []
            for source in range(gy):
                tall = frecv[piece][j, source].astype(F32)[:tallest]
                for i in range(nb):
                    part = tall[i * count : (i + 1) * count]
                    x.append(part + coupling(source, i) if joins else part)
            p, q = block_forward(x)
            pz, qz = {}, {}
            for k in range(blocks // 2):
                one, two = (p[k], q[k]) if k else (p[0], p[blocks // 2])
                y = jnp.concatenate([one, two], axis=1).astype(BF16)
                spec = jnp.dot(y, table[k], preferred_element_type=F32)
                filtered = (spec * gains[which, j, :, pl.ds(k * 2 * LANES, 2 * LANES)]).astype(BF16)
                z = lax.dot_general(filtered, table[k], (((1,), (1,)), ((), ())), preferred_element_type=F32)
                pz[k] = z[:, :LANES]
                if k:
                    qz[k] = z[:, LANES:]
                else:
                    pz[blocks // 2] = z[:, LANES:]
            back = block_backward(pz, qz)
            if joins:
                back = [part + coupling(a // nb, a % nb) for a, part in enumerate(back)]
            for way, row in enumerate(ends):
                if first <= row < first + count:
                    for owner in range(gy):
                        parts = [part[row - first : row - first + 1] for part in back[owner * nb : (owner + 1) * nb]]
                        esend[which, way, j, owner] = filled(jnp.concatenate(parts, axis=0), 8).astype(BF16)
                    for mask in [*masks, 0]:
                        other = flipped(h, mask, gy)
                        early.append(remote(
                            esend.at[which, way, j, other], erecv.at[which, way, j, h],
                            esend_sem.at[which, way, j, mask], erecv_sem.at[which, way, j, mask],
                            gx=sides[way], gy=other,
                        ))
            for owner in range(gy):
                tall = jnp.concatenate(back[owner * nb : (owner + 1) * nb], axis=0)
                bsend[piece][j, owner] = filled(tall, bsend[piece].shape[2]).astype(BF16)
            sent.append(exchange(bsend[piece], brecv[piece], bsend_sem[piece], brecv_sem[piece], j))
        return sent, early

    def updated(piece, j, owner):
        low, _, first, count, _ = pieces[piece]
        tall = brecv[piece][j, owner].astype(F32)
        wide = jnp.concatenate([tall[i * count : (i + 1) * count] for i in range(nb)], axis=1)
        return fields[low + j * gy + owner, pl.ds(first, count), :] + wide

    def send_raw_edges():
        for level in range(levels):
            for way, row in enumerate(ends):
                edges[way, pl.ds(level, 1), :] = fields[level, pl.ds(row, 1), :]
        return [
            remote(edges.at[way], halos.at[way], hsend_sem.at[way], hrecv_sem.at[way], gx=sides[way])
            for way in range(2)
        ]

    def finish_level(which, j, owner, values):
        level = owned[which][0] + j * gy + owner
        row = lax.broadcasted_iota(jnp.int32, (rows, cols), 0)
        keep = jnp.where(section == 1, land[...].astype(F32), 1.0)
        above = jnp.where(g == gx - 1, 0.0, 1.0)
        below = jnp.where(g == 0, 0.0, 1.0)
        after, before = halos[0, pl.ds(level, 1), :], halos[1, pl.ds(level, 1), :]
        returned = [erecv[which, way, j, owner].astype(F32) for way in range(2)]
        wide = [jnp.concatenate([tall[i : i + 1] for i in range(nb)], axis=1) for tall in returned]
        after, before = after + wide[0], before + wide[1]
        after = jnp.where(row == rows - 1, after * above, pltpu.roll(values, rows - 1, 0))
        before = jnp.where(row == 0, before * below, pltpu.roll(values, 1, 0))
        out_ref[level] = (values + rate[...] * (after + before - 2.0 * values)) * keep

    def cells(index):
        row = ((index.astype(F32) + 0.5) * np.float32(1.0 / cols)).astype(jnp.int32)
        return row, index - row * cols

    def gather_couplings():
        wide = 2 * LANES if cols % (2 * LANES) == 0 else LANES
        parts = cols // wide
        chunk = gy * slots
        surface = jnp.concatenate(
            [fields[c, :, pl.ds(i * wide, wide)] for c in range(FC) for i in range(parts)], axis=0
        ).astype(BF16)

        @pl.loop(0, gx)
        def _(way):
            base = way * gy
            index = jnp.concatenate([src_ref[pl.ds(base + i, 1), :] for i in range(gy)], axis=1)
            row, col = cells(index)
            part = col // wide
            pick = jnp.where(lax.broadcasted_iota(jnp.int32, (wide, chunk), 0) == col - part * wide, 1.0, 0.0)
            found = jnp.dot(surface, pick.astype(BF16), preferred_element_type=F32).reshape(FC, parts * rows, chunk)
            mine = (lax.broadcasted_iota(jnp.int32, (parts * rows, chunk), 0) == part * rows + row)[None]
            values = jnp.sum(jnp.where(mine, found, 0.0), axis=1)
            scaled = []
            for i in range(gy):
                slot = lax.broadcasted_iota(jnp.int32, (1, slots), 1)
                weight = jnp.where(slot < count_ref[base + i], weight_ref[pl.ds(base + i, 1), :], 0.0)
                scaled.append(values[:, i * slots : (i + 1) * slots] * weight)
            for c in range(FC):
                sendc[way * FC + c] = jnp.concatenate([part[c : c + 1] for part in scaled], axis=0).astype(BF16)

    def couple_copy(target):
        return pltpu.make_async_remote_copy(
            src_ref=sendc.at[target],
            dst_ref=recvc.at[me],
            send_sem=csend_sem,
            recv_sem=crecv_sem,
            device_id={"comp": 1 - section, "gx": target // FC, "gy": target % FC},
            device_id_type=MESH,
        )

    couplings = pltpu.make_async_remote_copy(
        src_ref=sendc, dst_ref=recvc, send_sem=csend_sem, recv_sem=crecv_sem,
        device_id={"comp": 1 - section}, device_id_type=MESH,
    )

    def land_couplings():
        couplings.wait_recv()
        per = CHUNK // slots
        landing[...] = dsts[...].astype(jnp.int32)
        for source in range(gy):
            def chunk_sum(c, total):
                base = c * per
                index = jnp.concatenate([landing[source, pl.ds(base + i, 1), :] for i in range(per)], axis=1)
                values = [recvc[base + i].astype(F32)[source : source + 1] for i in range(per)]
                values = jnp.concatenate(values, axis=1)
                row, col = cells(index)
                block = col // LANES
                mine = lax.broadcasted_iota(jnp.int32, (lines, CHUNK), 0) == block * rows + row
                lane = lax.broadcasted_iota(jnp.int32, (LANES, CHUNK), 0) == col - block * LANES
                return total + lax.dot_general(
                    jnp.where(mine, 1.0, 0.0).astype(BF16),
                    jnp.where(lane, values, 0.0).astype(BF16),
                    (((1,), (1,)), ((), ())),
                    preferred_element_type=F32,
                )

            landed[source] = lax.fori_loop(
                0, peers // per, chunk_sum, jnp.zeros((lines, LANES), F32), unroll=min(8, peers // per)
            )

    forward, backward = {}, {}
    load_high.wait()
    for piece in plain:
        pack_piece(piece)
    load_low.wait()
    for load_one in (load_src, load_weight, load_count):
        load_one.wait()
    gather_couplings()
    for piece in coupled:
        pack_piece(piece)
    load_dst.wait()
    short[...] = dst_ref[...].astype(jnp.int16)
    pl.semaphore_wait(barrier, gy - 1 + peers + 2 * gy)
    indices = []
    for mask in masks:
        other = flipped(h, mask, gy)
        indices.append(remote(short, dsts.at[h], isend_sem.at[mask], irecv_sem.at[mask], gy=other))
    dsts[h] = short[...]

    @pl.loop(0, gx * FC)
    def _(target):
        couple_copy(target).start()

    for piece in plain:
        forward[piece] = send_forward(piece)
    for piece in coupled:
        forward[piece] = send_forward(piece)
    halo = send_raw_edges()
    load_place = load(place_hbm, place, 6)
    load_resp = load(resp_hbm, resp, 7)
    load_table = load(table_hbm, table, 8)
    load_rate = load(rate_hbm, rate, 9)
    load_land = load(land_hbm, land, 10)
    load_place.wait()
    load_resp.wait()
    expand_gains()
    load_table.wait()
    for piece in plain:
        backward[piece] = transform(piece, forward[piece])
    for copy in indices:
        copy.wait_recv()
    if FC == gy:
        land_couplings()
    else:
        pl.when(h < FC)(land_couplings)

        @pl.when(h >= FC)
        def _():
            landed[...] = jnp.zeros_like(landed)

    for piece in coupled:
        backward[piece] = transform(piece, forward[piece])
    load_rate.wait()
    load_land.wait()
    for copy in halo:
        copy.wait_recv()
    for which in range(len(owned)):
        group = [piece for piece in range(len(pieces)) if pieces[piece][4] == which]
        for piece in group:
            for copy in backward[piece][1]:
                copy.wait_recv()
        for j in counts(group[0]):
            for mask in [0, *reversed(masks)]:
                owner = flipped(h, mask, gy)
                for piece in group:
                    if mask:
                        backward[piece][0][j][mask].wait_recv()
                finish_level(which, j, owner, jnp.concatenate([updated(piece, j, owner) for piece in group], axis=0))
    couplings.wait_send()
    for copy in leaving:
        copy.wait_send()


def local(state, response, diffusion, land_mask, couple_src, couple_dst, couple_weight, couple_count):
    levels, rows, cols = state.shape[1:]
    gx, gy = lax.axis_size("gx"), lax.axis_size("gy")
    peers, slots = couple_src.shape[3:]
    cols_all = cols * gy
    nb, blocks = cols // LANES, cols_all // LANES
    lines = nb * rows
    pieces = phases(levels, rows, gy)
    owned = owned_sets(levels, gy)
    many = max(count for _, count in owned)
    tables = jnp.asarray(lane_tables(cols_all))
    places = jnp.asarray(spread_table(blocks))
    hbm = pl.BlockSpec(memory_space=pltpu.HBM)
    stay = lambda value: pltpu.with_memory_space_constraint(value, pltpu.HBM)
    dma = pltpu.SemaphoreType.DMA
    messages = [
        ((high - low) // gy, gy, -(-(nb * count) // 16) * 16, LANES) for low, high, _, count, _ in pieces
    ]
    out = pl.pallas_call(
        functools.partial(kernel, gx, gy, pieces),
        out_shape=jax.ShapeDtypeStruct((levels, rows, cols), F32),
        in_specs=[hbm] * 10,
        out_specs=pl.BlockSpec(memory_space=pltpu.VMEM),
        scratch_shapes=[
            pltpu.VMEM((levels, rows, cols), F32),
            pltpu.VMEM(tables.shape, BF16),
            pltpu.VMEM(places.shape, BF16),
            pltpu.VMEM((levels, cols_all), F32),
            pltpu.VMEM((len(owned), many, 1, cols_all), F32),
            pltpu.VMEM((rows, cols), F32),
            pltpu.VMEM((rows, cols), jnp.int32),
            pltpu.VMEM((peers, slots), jnp.int32),
            pltpu.VMEM((peers, slots), jnp.int32),
            pltpu.VMEM((peers, slots), F32),
            pltpu.SMEM((peers,), jnp.int32),
            pltpu.VMEM((gx * FC, gy, slots), BF16),
            pltpu.VMEM((peers, gy, slots), BF16),
            pltpu.VMEM((peers, slots), jnp.int16),
            pltpu.VMEM((gy, peers, slots), jnp.int16),
            pltpu.VMEM((gy, peers, slots), jnp.int32),
            pltpu.VMEM((gy, lines, LANES), F32),
            pltpu.VMEM((len(owned), 2, many, gy, 8, LANES), BF16),
            pltpu.VMEM((len(owned), 2, many, gy, 8, LANES), BF16),
            pltpu.VMEM((2, levels, cols), F32),
            pltpu.VMEM((2, levels, cols), F32),
            dma((11,)),
            dma,
            dma,
            dma((gy,)),
            dma((gy,)),
            dma((len(owned), 2, many, gy)),
            dma((len(owned), 2, many, gy)),
            dma((2,)),
            dma((2,)),
            *[pltpu.VMEM(message, BF16) for _ in range(4) for message in messages],
            *[dma(message[:2]) for _ in range(4) for message in messages],
        ],
        compiler_params=pltpu.CompilerParams(
            collective_id=0, has_side_effects=True, vmem_limit_bytes=48 * 1024 * 1024
        ),
    )(
        *map(
            stay,
            (
                state[0],
                response[0],
                diffusion[0],
                land_mask,
                couple_src.reshape(peers, slots),
                couple_dst.reshape(peers, slots),
                couple_weight.reshape(peers, slots),
                couple_count.reshape(peers),
                tables,
                places,
            ),
        )
    )
    return out[None]


def solution(mesh):
    return jax.shard_map(
        local,
        mesh=mesh,
        in_specs=(
            P("comp", None, "gx", "gy"),
            P("comp", None, None),
            P("comp", "gx", "gy"),
            P("gx", "gy"),
            P("comp", "gx", "gy", None, None),
            P("comp", "gx", "gy", None, None),
            P("comp", "gx", "gy", None, None),
            P("comp", "gx", "gy", None),
        ),
        out_specs=P("comp", None, "gx", "gy"),
        check_vma=False,
    )
```

```python
import functools
import math

import jax
import jax.numpy as jnp
import ml_dtypes
import numpy as np
from jax import lax
from jax.experimental import pallas as pl
from jax.experimental.pallas import tpu as pltpu
from jax.sharding import PartitionSpec as P

FC = 4
LANES = 128
CHUNK = 256
CUT = 24
MESH = pl.DeviceIdType.MESH
F32 = jnp.float32
BF16 = jnp.bfloat16


def lane_tables(cols):
    blocks = cols // LANES
    lane = np.arange(LANES)[:, None]
    step = np.arange(LANES // 2)[None, :]
    tables = np.zeros((blocks // 2, 2 * LANES, 2 * LANES), np.float64)
    for k in range(blocks // 2):
        for place, residue in enumerate((k, blocks - k) if k else (0, blocks // 2)):
            angle = 2.0 * math.pi / cols * (lane * (blocks * step + residue) % cols)
            cos, sin = np.cos(angle), np.sin(angle)
            span = slice(place * LANES, (place + 1) * LANES)
            if k:
                sign = -1.0 if place else 1.0
                tables[k, :LANES, span] = np.concatenate([cos, sin], axis=1)
                tables[k, LANES:, span] = np.concatenate([-sin, cos], axis=1) * sign
            else:
                tables[k, span, span] = np.concatenate([cos, sin], axis=1)
    return tables.astype(ml_dtypes.bfloat16)


def pair_order(blocks):
    order = [0, blocks // 2]
    for k in range(1, blocks // 2):
        order += [k, blocks - k]
    return order


def spread_table(blocks):
    table = np.zeros((blocks * 16, blocks * LANES), np.float32)
    for place, residue in enumerate(pair_order(blocks)):
        for lane in range(LANES):
            table[blocks * (lane % 16) + residue, place * LANES + lane] = 1.0
    return table.astype(ml_dtypes.bfloat16)


def weighted(terms):
    total = None
    for coef, value in terms:
        if abs(coef) < 1e-12:
            continue
        if abs(abs(coef) - 1.0) < 1e-12:
            if total is None:
                total = value if coef > 0 else -value
            else:
                total = total + value if coef > 0 else total - value
        else:
            scaled = value * np.float32(coef)
            total = scaled if total is None else total + scaled
    return total


def block_forward(x):
    n = len(x)
    half, quarter = n // 2, n // 4
    cos = lambda a, k: math.cos(2.0 * math.pi * (a * k % n) / n)
    sin = lambda a, k: math.sin(2.0 * math.pi * (a * k % n) / n)
    even = {a: x[a] + x[n - a] for a in range(1, half)}
    odd = {a: x[a] - x[n - a] for a in range(1, half)}
    even[0], even[half] = x[0], x[half]
    ee = {a: even[a] + even[half - a] for a in range(quarter)}
    eo = {a: even[a] - even[half - a] for a in range(quarter)}
    ee[quarter] = even[quarter]
    oe = {a: odd[a] - odd[half - a] for a in range(1, quarter)}
    oo = {a: odd[a] + odd[half - a] for a in range(1, quarter)}
    oo[quarter] = odd[quarter]
    p, q = {}, {}
    for k in range(half + 1):
        p[k] = weighted([(cos(a, k), v) for a, v in (eo if k % 2 else ee).items()])
        if 0 < k < half:
            q[k] = weighted([(sin(a, k), v) for a, v in (oo if k % 2 else oe).items()])
    return p, q


def block_backward(p, q):
    half = max(p)
    n, quarter = 2 * half, half // 2
    cos = lambda a, k: math.cos(2.0 * math.pi * (a * k % n) / n)
    sin = lambda a, k: math.sin(2.0 * math.pi * (a * k % n) / n)
    u, v = {}, {}
    for a in range(quarter + 1):
        ue = weighted([(cos(a, k), p[k]) for k in range(0, half + 1, 2)])
        uo = weighted([(cos(a, k), p[k]) for k in range(1, half + 1, 2)])
        if a == quarter:
            u[a] = ue
        else:
            u[a], u[half - a] = ue + uo, ue - uo
        if a:
            vo = weighted([(sin(a, k), q[k]) for k in range(1, half, 2)])
            if a == quarter:
                v[a] = vo
            else:
                ve = weighted([(sin(a, k), q[k]) for k in range(2, half, 2)])
                v[a], v[half - a] = vo + ve, vo - ve
    x = [None] * n
    x[0], x[half] = u[0], u[half]
    for a in range(1, half):
        x[a], x[n - a] = u[a] + v[a], u[a] - v[a]
    return x


def flipped(index, mask, size):
    total, bit = 0, 1
    while bit < size:
        digit = (index // bit) % 2
        total = total + bit * (1 - digit if mask & bit else digit)
        bit *= 2
    return total


def far_first(size):
    return sorted(range(1, size), key=lambda mask: (mask < size // 2, mask))


def phases(levels, rows, groups_y):
    if FC % groups_y == 0 and (levels - FC) % groups_y == 0:
        cut = CUT if rows > CUT else rows
        pieces = [(FC, levels, 0, rows, 0), (0, FC, 0, cut, 1)]
        return pieces + ([(0, FC, cut, rows - cut, 1)] if cut < rows else [])
    return [(0, levels, 0, rows, 0)]


def owned_sets(levels, groups_y):
    sets = {}
    for low, high, _, _, which in phases(levels, 1, groups_y):
        sets[which] = (low, (high - low) // groups_y)
    return [sets[which] for which in sorted(sets)]


class Guarded:
    def __init__(self, copy, sends, receives):
        self.copy, self.sends, self.receives = copy, sends, receives
        pl.when(sends)(lambda: copy.start())

    def wait_send(self):
        pl.when(self.sends)(lambda: self.copy.wait_send())

    def wait_recv(self):
        pl.when(self.receives)(lambda: self.copy.wait_recv())


def kernel(
    gx, gy, pieces, state_hbm, resp_hbm, rate_hbm, land_hbm, src_hbm, dst_hbm, weight_hbm, count_hbm, table_hbm, place_hbm,
    out_ref,
    fields, table, place, resp, gains, rate, land, src_ref, dst_ref, weight_ref, count_ref,
    sendc, recvc, short, dsts, landing, landed, esend, erecv, edges, halos,
    load_sem, csend_sem, crecv_sem, isend_sem, irecv_sem, esend_sem, erecv_sem, hsend_sem, hrecv_sem,
    *buffers,
):
    fsend, frecv, bsend, brecv, fsend_sem, frecv_sem, bsend_sem, brecv_sem = (
        buffers[i * len(pieces) : (i + 1) * len(pieces)] for i in range(8)
    )
    levels, rows, cols = fields.shape
    peers, slots = src_ref.shape
    nb = cols // LANES
    lines = nb * rows
    blocks = nb * gy
    owned = owned_sets(levels, gy)
    coupled = [piece for piece in range(len(pieces)) if pieces[piece][0] == 0]
    plain = [piece for piece in range(len(pieces)) if pieces[piece][0] > 0]
    section = lax.axis_index("comp")
    g = lax.axis_index("gx")
    h = lax.axis_index("gy")
    me = g * gy + h
    sides = ((g + gx - 1) % gx, (g + 1) % gx)
    ends = (0, rows - 1)
    masks = far_first(gy)
    leaving = []

    def load(source, target, at):
        copy = pltpu.make_async_copy(source, target, load_sem.at[at])
        copy.start()
        return copy

    load_high = load(state_hbm.at[pl.ds(FC, levels - FC)], fields.at[pl.ds(FC, levels - FC)], 0)
    load_low = load(state_hbm.at[pl.ds(0, FC)], fields.at[pl.ds(0, FC)], 1)

    load_dst = load(dst_hbm, dst_ref, 5)

    barrier = pltpu.get_barrier_semaphore()

    def greet(**device):
        pl.semaphore_signal(barrier, inc=1, device_id=device, device_id_type=MESH)

    for mask in masks:
        greet(gy=flipped(h, mask, gy))

    @pl.loop(0, peers)
    def _(q):
        greet(comp=1 - section, gx=q // gy, gy=q % gy)

    for side in sides:
        for mask in [*masks, 0]:
            greet(gx=side, gy=flipped(h, mask, gy))

    load_src = load(src_hbm, src_ref, 2)
    load_weight = load(weight_hbm, weight_ref, 3)
    load_count = load(count_hbm, count_ref, 4)

    def filled(tall, count):
        if count > tall.shape[0]:
            tall = jnp.concatenate([tall, jnp.zeros((count - tall.shape[0], LANES), F32)], axis=0)
        return tall

    def remote(source, target, send_sem, recv_sem, way=None, **device):
        copy = pltpu.make_async_remote_copy(
            src_ref=source,
            dst_ref=target,
            send_sem=send_sem,
            recv_sem=recv_sem,
            device_id=device,
            device_id_type=MESH,
        )
        if way is None:
            copy.start()
        else:
            copy = Guarded(copy, *((g > 0, g < gx - 1) if way == 0 else (g < gx - 1, g > 0)))
        leaving.append(copy)
        return copy

    def exchange(source, target, send_sem, recv_sem, j):
        copies = {}
        for mask in masks:
            other = flipped(h, mask, gy)
            copies[mask] = remote(
                source.at[j, other], target.at[j, h], send_sem.at[j, mask], recv_sem.at[j, mask], gy=other
            )
        target[j, h] = source[j, h]
        return copies

    def counts(piece):
        low, high = pieces[piece][:2]
        return range((high - low) // gy)

    def pack_piece(piece):
        low, _, first, count, _ = pieces[piece]
        for j in counts(piece):
            for owner in range(gy):
                values = fields[low + j * gy + owner, pl.ds(first, count), :]
                tall = jnp.concatenate([values[:, i * LANES : (i + 1) * LANES] for i in range(nb)], axis=0)
                fsend[piece][j, owner] = filled(tall, fsend[piece].shape[2]).astype(BF16)

    def send_forward(piece):
        return [exchange(fsend[piece], frecv[piece], fsend_sem[piece], frecv_sem[piece], j) for j in counts(piece)]

    def expand_gains():
        groups, width = LANES // 16, blocks * 16
        rows_all = []
        for low, many in owned:
            for j in range(many):
                line = resp[pl.ds(low + j * gy + h, 1), :] * np.float32(2.0 / (groups * width))
                rows_all.append(jnp.concatenate([line[:, i * width : (i + 1) * width] for i in range(groups)], axis=0))
        values = jnp.concatenate(rows_all, axis=0)
        count = values.shape[0]
        top = values.astype(BF16)
        rest = (values - top.astype(F32)).astype(BF16)
        both = jnp.concatenate([top, rest], axis=0)
        lane = lax.broadcasted_iota(jnp.int32, (groups, 2 * LANES), 1) % LANES
        mine = lane // 16 == lax.broadcasted_iota(jnp.int32, (groups, 2 * LANES), 0)
        for k in range(blocks // 2):
            span = pl.ds(k * 2 * LANES, 2 * LANES)
            wide = jnp.dot(both, place[:, span], preferred_element_type=F32)
            wide = wide[:count] + wide[count:]
            at = 0
            for which, (_, many) in enumerate(owned):
                for j in range(many):
                    mixed = jnp.where(mine, wide[at : at + groups], 0.0)
                    gains[which, j, :, span] = jnp.sum(mixed, axis=0, keepdims=True)
                    at += groups

    def transform(piece, arriving):
        _, _, first, count, which = pieces[piece]
        tallest = nb * count
        sent, early = [], []
        for j in counts(piece):
            for copy in arriving[j].values():
                copy.wait_recv()
            joins = piece in coupled and j == 0

            def coupling(source, i):
                return landed[source, pl.ds(i * rows + first, count), :]

            x = []
            for source in range(gy):
                tall = frecv[piece][j, source].astype(F32)[:tallest]
                for i in range(nb):
                    part = tall[i * count : (i + 1) * count]
                    x.append(part + coupling(source, i) if joins else part)
            p, q = block_forward(x)
            pz, qz = {}, {}
            for k in range(blocks // 2):
                one, two = (p[k], q[k]) if k else (p[0], p[blocks // 2])
                y = jnp.concatenate([one, two], axis=1).astype(BF16)
                spec = jnp.dot(y, table[k], preferred_element_type=F32)
                filtered = (spec * gains[which, j, :, pl.ds(k * 2 * LANES, 2 * LANES)]).astype(BF16)
                z = lax.dot_general(filtered, table[k], (((1,), (1,)), ((), ())), preferred_element_type=F32)
                pz[k] = z[:, :LANES]
                if k:
                    qz[k] = z[:, LANES:]
                else:
                    pz[blocks // 2] = z[:, LANES:]
            back = block_backward(pz, qz)
            if joins:
                back = [part + coupling(a // nb, a % nb) for a, part in enumerate(back)]
            for way, row in enumerate(ends):
                if first <= row < first + count:
                    for owner in range(gy):
                        parts = [part[row - first : row - first + 1] for part in back[owner * nb : (owner + 1) * nb]]
                        esend[which, way, j, owner] = filled(jnp.concatenate(parts, axis=0), 8).astype(BF16)
                    for mask in [*masks, 0]:
                        other = flipped(h, mask, gy)
                        early.append(remote(
                            esend.at[which, way, j, other], erecv.at[which, way, j, h],
                            esend_sem.at[which, way, j, mask], erecv_sem.at[which, way, j, mask],
                            way=way, gx=sides[way], gy=other,
                        ))
            for owner in range(gy):
                tall = jnp.concatenate(back[owner * nb : (owner + 1) * nb], axis=0)
                bsend[piece][j, owner] = filled(tall, bsend[piece].shape[2]).astype(BF16)
            sent.append(exchange(bsend[piece], brecv[piece], bsend_sem[piece], brecv_sem[piece], j))
        return sent, early

    def updated(piece, j, owner):
        low, _, first, count, _ = pieces[piece]
        tall = brecv[piece][j, owner].astype(F32)
        wide = jnp.concatenate([tall[i * count : (i + 1) * count] for i in range(nb)], axis=1)
        return fields[low + j * gy + owner, pl.ds(first, count), :] + wide

    def send_raw_edges():
        for level in range(levels):
            for way, row in enumerate(ends):
                edges[way, pl.ds(level, 1), :] = fields[level, pl.ds(row, 1), :]
        return [
            remote(edges.at[way], halos.at[way], hsend_sem.at[way], hrecv_sem.at[way], way=way, gx=sides[way])
            for way in range(2)
        ]

    def finish_level(which, j, owner, values):
        level = owned[which][0] + j * gy + owner
        row = lax.broadcasted_iota(jnp.int32, (rows, cols), 0)
        keep = jnp.where(section == 1, land[...].astype(F32), 1.0)
        above = jnp.where(g == gx - 1, 0.0, 1.0)
        below = jnp.where(g == 0, 0.0, 1.0)
        after, before = halos[0, pl.ds(level, 1), :], halos[1, pl.ds(level, 1), :]
        returned = [erecv[which, way, j, owner].astype(F32) for way in range(2)]
        wide = [jnp.concatenate([tall[i : i + 1] for i in range(nb)], axis=1) for tall in returned]
        after, before = after + wide[0], before + wide[1]
        after = jnp.where(row == rows - 1, after * above, pltpu.roll(values, rows - 1, 0))
        before = jnp.where(row == 0, before * below, pltpu.roll(values, 1, 0))
        out_ref[level] = (values + rate[...] * (after + before - 2.0 * values)) * keep

    def cells(index):
        row = ((index.astype(F32) + 0.5) * np.float32(1.0 / cols)).astype(jnp.int32)
        return row, index - row * cols

    def gather_couplings():
        wide = 2 * LANES if cols % (2 * LANES) == 0 else LANES
        parts = cols // wide
        chunk = gy * slots
        surface = jnp.concatenate(
            [fields[c, :, pl.ds(i * wide, wide)] for c in range(FC) for i in range(parts)], axis=0
        ).astype(BF16)

        @pl.loop(0, gx)
        def _(way):
            base = way * gy
            index = jnp.concatenate([src_ref[pl.ds(base + i, 1), :] for i in range(gy)], axis=1)
            row, col = cells(index)
            part = col // wide
            pick = jnp.where(lax.broadcasted_iota(jnp.int32, (wide, chunk), 0) == col - part * wide, 1.0, 0.0)
            found = jnp.dot(surface, pick.astype(BF16), preferred_element_type=F32).reshape(FC, parts * rows, chunk)
            mine = (lax.broadcasted_iota(jnp.int32, (parts * rows, chunk), 0) == part * rows + row)[None]
            values = jnp.sum(jnp.where(mine, found, 0.0), axis=1)
            scaled = []
            for i in range(gy):
                slot = lax.broadcasted_iota(jnp.int32, (1, slots), 1)
                weight = jnp.where(slot < count_ref[base + i], weight_ref[pl.ds(base + i, 1), :], 0.0)
                scaled.append(values[:, i * slots : (i + 1) * slots] * weight)
            for c in range(FC):
                sendc[way * FC + c] = jnp.concatenate([part[c : c + 1] for part in scaled], axis=0).astype(BF16)

    def couple_copy(target):
        return pltpu.make_async_remote_copy(
            src_ref=sendc.at[target],
            dst_ref=recvc.at[me],
            send_sem=csend_sem,
            recv_sem=crecv_sem,
            device_id={"comp": 1 - section, "gx": target // FC, "gy": target % FC},
            device_id_type=MESH,
        )

    couplings = pltpu.make_async_remote_copy(
        src_ref=sendc, dst_ref=recvc, send_sem=csend_sem, recv_sem=crecv_sem,
        device_id={"comp": 1 - section}, device_id_type=MESH,
    )

    def land_couplings():
        couplings.wait_recv()
        per = CHUNK // slots
        landing[...] = dsts[...].astype(jnp.int32)
        for source in range(gy):
            def chunk_sum(c, total):
                base = c * per
                index = jnp.concatenate([landing[source, pl.ds(base + i, 1), :] for i in range(per)], axis=1)
                values = [recvc[base + i].astype(F32)[source : source + 1] for i in range(per)]
                values = jnp.concatenate(values, axis=1)
                row, col = cells(index)
                block = col // LANES
                mine = lax.broadcasted_iota(jnp.int32, (lines, CHUNK), 0) == block * rows + row
                lane = lax.broadcasted_iota(jnp.int32, (LANES, CHUNK), 0) == col - block * LANES
                return total + lax.dot_general(
                    jnp.where(mine, 1.0, 0.0).astype(BF16),
                    jnp.where(lane, values, 0.0).astype(BF16),
                    (((1,), (1,)), ((), ())),
                    preferred_element_type=F32,
                )

            landed[source] = lax.fori_loop(
                0, peers // per, chunk_sum, jnp.zeros((lines, LANES), F32), unroll=min(8, peers // per)
            )

    for way, border in enumerate((gx - 1, 0)):
        @pl.when(g == border)
        def _(way=way):
            halos[way] = jnp.zeros(halos.shape[1:], F32)
            erecv[:, way] = jnp.zeros((erecv.shape[0], *erecv.shape[2:]), BF16)

    forward, backward = {}, {}
    load_high.wait()
    for piece in plain:
        pack_piece(piece)
    load_low.wait()
    for load_one in (load_src, load_weight, load_count):
        load_one.wait()
    gather_couplings()
    for piece in coupled:
        pack_piece(piece)
    load_dst.wait()
    short[...] = dst_ref[...].astype(jnp.int16)
    pl.semaphore_wait(barrier, gy - 1 + peers + 2 * gy)
    indices = []
    for mask in masks:
        other = flipped(h, mask, gy)
        indices.append(remote(short, dsts.at[h], isend_sem.at[mask], irecv_sem.at[mask], gy=other))
    dsts[h] = short[...]

    @pl.loop(0, gx * FC)
    def _(target):
        couple_copy(target).start()

    for piece in plain:
        forward[piece] = send_forward(piece)
    for piece in coupled:
        forward[piece] = send_forward(piece)
    halo = send_raw_edges()
    load_place = load(place_hbm, place, 6)
    load_resp = load(resp_hbm, resp, 7)
    load_table = load(table_hbm, table, 8)
    load_rate = load(rate_hbm, rate, 9)
    load_land = load(land_hbm, land, 10)
    load_place.wait()
    load_resp.wait()
    expand_gains()
    load_table.wait()
    for piece in plain:
        backward[piece] = transform(piece, forward[piece])
    for copy in indices:
        copy.wait_recv()
    if FC == gy:
        land_couplings()
    else:
        pl.when(h < FC)(land_couplings)

        @pl.when(h >= FC)
        def _():
            landed[...] = jnp.zeros_like(landed)

    for piece in coupled:
        backward[piece] = transform(piece, forward[piece])
    load_rate.wait()
    load_land.wait()
    for copy in halo:
        copy.wait_recv()
    for which in range(len(owned)):
        group = [piece for piece in range(len(pieces)) if pieces[piece][4] == which]
        for piece in group:
            for copy in backward[piece][1]:
                copy.wait_recv()
        for j in counts(group[0]):
            for mask in [0, *reversed(masks)]:
                owner = flipped(h, mask, gy)
                for piece in group:
                    if mask:
                        backward[piece][0][j][mask].wait_recv()
                finish_level(which, j, owner, jnp.concatenate([updated(piece, j, owner) for piece in group], axis=0))
    couplings.wait_send()
    for copy in leaving:
        copy.wait_send()


def local(state, response, diffusion, land_mask, couple_src, couple_dst, couple_weight, couple_count):
    levels, rows, cols = state.shape[1:]
    gx, gy = lax.axis_size("gx"), lax.axis_size("gy")
    peers, slots = couple_src.shape[3:]
    cols_all = cols * gy
    nb, blocks = cols // LANES, cols_all // LANES
    lines = nb * rows
    pieces = phases(levels, rows, gy)
    owned = owned_sets(levels, gy)
    many = max(count for _, count in owned)
    tables = jnp.asarray(lane_tables(cols_all))
    places = jnp.asarray(spread_table(blocks))
    hbm = pl.BlockSpec(memory_space=pltpu.HBM)
    stay = lambda value: pltpu.with_memory_space_constraint(value, pltpu.HBM)
    dma = pltpu.SemaphoreType.DMA
    messages = [
        ((high - low) // gy, gy, -(-(nb * count) // 16) * 16, LANES) for low, high, _, count, _ in pieces
    ]
    out = pl.pallas_call(
        functools.partial(kernel, gx, gy, pieces),
        out_shape=jax.ShapeDtypeStruct((levels, rows, cols), F32),
        in_specs=[hbm] * 10,
        out_specs=pl.BlockSpec(memory_space=pltpu.VMEM),
        scratch_shapes=[
            pltpu.VMEM((levels, rows, cols), F32),
            pltpu.VMEM(tables.shape, BF16),
            pltpu.VMEM(places.shape, BF16),
            pltpu.VMEM((levels, cols_all), F32),
            pltpu.VMEM((len(owned), many, 1, cols_all), F32),
            pltpu.VMEM((rows, cols), F32),
            pltpu.VMEM((rows, cols), jnp.int32),
            pltpu.VMEM((peers, slots), jnp.int32),
            pltpu.VMEM((peers, slots), jnp.int32),
            pltpu.VMEM((peers, slots), F32),
            pltpu.SMEM((peers,), jnp.int32),
            pltpu.VMEM((gx * FC, gy, slots), BF16),
            pltpu.VMEM((peers, gy, slots), BF16),
            pltpu.VMEM((peers, slots), jnp.int16),
            pltpu.VMEM((gy, peers, slots), jnp.int16),
            pltpu.VMEM((gy, peers, slots), jnp.int32),
            pltpu.VMEM((gy, lines, LANES), F32),
            pltpu.VMEM((len(owned), 2, many, gy, 8, LANES), BF16),
            pltpu.VMEM((len(owned), 2, many, gy, 8, LANES), BF16),
            pltpu.VMEM((2, levels, cols), F32),
            pltpu.VMEM((2, levels, cols), F32),
            dma((11,)),
            dma,
            dma,
            dma((gy,)),
            dma((gy,)),
            dma((len(owned), 2, many, gy)),
            dma((len(owned), 2, many, gy)),
            dma((2,)),
            dma((2,)),
            *[pltpu.VMEM(message, BF16) for _ in range(4) for message in messages],
            *[dma(message[:2]) for _ in range(4) for message in messages],
        ],
        compiler_params=pltpu.CompilerParams(
            collective_id=0, has_side_effects=True, vmem_limit_bytes=48 * 1024 * 1024
        ),
    )(
        *map(
            stay,
            (
                state[0],
                response[0],
                diffusion[0],
                land_mask,
                couple_src.reshape(peers, slots),
                couple_dst.reshape(peers, slots),
                couple_weight.reshape(peers, slots),
                couple_count.reshape(peers),
                tables,
                places,
            ),
        )
    )
    return out[None]


def solution(mesh):
    return jax.shard_map(
        local,
        mesh=mesh,
        in_specs=(
            P("comp", None, "gx", "gy"),
            P("comp", None, None),
            P("comp", "gx", "gy"),
            P("gx", "gy"),
            P("comp", "gx", "gy", None, None),
            P("comp", "gx", "gy", None, None),
            P("comp", "gx", "gy", None, None),
            P("comp", "gx", "gy", None),
        ),
        out_specs=P("comp", None, "gx", "gy"),
        check_vma=False,
    )
```

```python
import functools
import math

import jax
import jax.numpy as jnp
import ml_dtypes
import numpy as np
from jax import lax
from jax.experimental import pallas as pl
from jax.experimental.pallas import tpu as pltpu
from jax.sharding import PartitionSpec as P

FC = 4
LANES = 128
CHUNK = 256
CUT = 24
MESH = pl.DeviceIdType.MESH
F32 = jnp.float32
BF16 = jnp.bfloat16


def lane_tables(cols):
    blocks = cols // LANES
    lane = np.arange(LANES)[:, None]
    step = np.arange(LANES // 2)[None, :]
    tables = np.zeros((blocks // 2, 2 * LANES, 2 * LANES), np.float64)
    for k in range(blocks // 2):
        for place, residue in enumerate((k, blocks - k) if k else (0, blocks // 2)):
            angle = 2.0 * math.pi / cols * (lane * (blocks * step + residue) % cols)
            cos, sin = np.cos(angle), np.sin(angle)
            span = slice(place * LANES, (place + 1) * LANES)
            if k:
                sign = -1.0 if place else 1.0
                tables[k, :LANES, span] = np.concatenate([cos, sin], axis=1)
                tables[k, LANES:, span] = np.concatenate([-sin, cos], axis=1) * sign
            else:
                tables[k, span, span] = np.concatenate([cos, sin], axis=1)
    return tables.astype(ml_dtypes.bfloat16)


def pair_order(blocks):
    order = [0, blocks // 2]
    for k in range(1, blocks // 2):
        order += [k, blocks - k]
    return order


def spread_table(blocks):
    table = np.zeros((blocks * 16, blocks * LANES), np.float32)
    for place, residue in enumerate(pair_order(blocks)):
        for lane in range(LANES):
            table[blocks * (lane % 16) + residue, place * LANES + lane] = 1.0
    return table.astype(ml_dtypes.bfloat16)


def weighted(terms):
    total = None
    for coef, value in terms:
        if abs(coef) < 1e-12:
            continue
        if abs(abs(coef) - 1.0) < 1e-12:
            if total is None:
                total = value if coef > 0 else -value
            else:
                total = total + value if coef > 0 else total - value
        else:
            scaled = value * np.float32(coef)
            total = scaled if total is None else total + scaled
    return total


def block_forward(x):
    n = len(x)
    half, quarter = n // 2, n // 4
    cos = lambda a, k: math.cos(2.0 * math.pi * (a * k % n) / n)
    sin = lambda a, k: math.sin(2.0 * math.pi * (a * k % n) / n)
    even = {a: x[a] + x[n - a] for a in range(1, half)}
    odd = {a: x[a] - x[n - a] for a in range(1, half)}
    even[0], even[half] = x[0], x[half]
    ee = {a: even[a] + even[half - a] for a in range(quarter)}
    eo = {a: even[a] - even[half - a] for a in range(quarter)}
    ee[quarter] = even[quarter]
    oe = {a: odd[a] - odd[half - a] for a in range(1, quarter)}
    oo = {a: odd[a] + odd[half - a] for a in range(1, quarter)}
    oo[quarter] = odd[quarter]
    p, q = {}, {}
    for k in range(half + 1):
        p[k] = weighted([(cos(a, k), v) for a, v in (eo if k % 2 else ee).items()])
        if 0 < k < half:
            q[k] = weighted([(sin(a, k), v) for a, v in (oo if k % 2 else oe).items()])
    return p, q


def block_backward(p, q):
    half = max(p)
    n, quarter = 2 * half, half // 2
    cos = lambda a, k: math.cos(2.0 * math.pi * (a * k % n) / n)
    sin = lambda a, k: math.sin(2.0 * math.pi * (a * k % n) / n)
    u, v = {}, {}
    for a in range(quarter + 1):
        ue = weighted([(cos(a, k), p[k]) for k in range(0, half + 1, 2)])
        uo = weighted([(cos(a, k), p[k]) for k in range(1, half + 1, 2)])
        if a == quarter:
            u[a] = ue
        else:
            u[a], u[half - a] = ue + uo, ue - uo
        if a:
            vo = weighted([(sin(a, k), q[k]) for k in range(1, half, 2)])
            if a == quarter:
                v[a] = vo
            else:
                ve = weighted([(sin(a, k), q[k]) for k in range(2, half, 2)])
                v[a], v[half - a] = vo + ve, vo - ve
    x = [None] * n
    x[0], x[half] = u[0], u[half]
    for a in range(1, half):
        x[a], x[n - a] = u[a] + v[a], u[a] - v[a]
    return x


def flipped(index, mask, size):
    total, bit = 0, 1
    while bit < size:
        digit = (index // bit) % 2
        total = total + bit * (1 - digit if mask & bit else digit)
        bit *= 2
    return total


def far_first(size):
    return sorted(range(1, size), key=lambda mask: (mask < size // 2, mask))


def phases(levels, rows, groups_y):
    if FC % groups_y == 0 and (levels - FC) % groups_y == 0:
        cut = CUT if rows > CUT else rows
        pieces = [(FC, levels, 0, rows, 0), (0, FC, 0, cut, 1)]
        return pieces + ([(0, FC, cut, rows - cut, 1)] if cut < rows else [])
    return [(0, levels, 0, rows, 0)]


def owned_sets(levels, groups_y):
    sets = {}
    for low, high, _, _, which in phases(levels, 1, groups_y):
        sets[which] = (low, (high - low) // groups_y)
    return [sets[which] for which in sorted(sets)]


class Guarded:
    def __init__(self, copy, sends, receives):
        self.copy, self.sends, self.receives = copy, sends, receives
        pl.when(sends)(lambda: copy.start())

    def wait_send(self):
        pl.when(self.sends)(lambda: self.copy.wait_send())

    def wait_recv(self):
        pl.when(self.receives)(lambda: self.copy.wait_recv())


def kernel(
    gx, gy, pieces, state_hbm, resp_hbm, rate_hbm, land_hbm, src_hbm, dst_hbm, weight_hbm, count_hbm, table_hbm, place_hbm,
    out_ref,
    fields, table, place, resp, gains, rate, land, src_ref, dst_ref, weight_ref, count_ref,
    sendc, recvc, short, dsts, landing, landed, esend, erecv, edges, halos,
    load_sem, csend_sem, crecv_sem, isend_sem, irecv_sem, esend_sem, erecv_sem, hsend_sem, hrecv_sem,
    *buffers,
):
    fsend, frecv, bsend, brecv, fsend_sem, frecv_sem, bsend_sem, brecv_sem = (
        buffers[i * len(pieces) : (i + 1) * len(pieces)] for i in range(8)
    )
    levels, rows, cols = fields.shape
    peers, slots = src_ref.shape
    nb = cols // LANES
    lines = nb * rows
    blocks = nb * gy
    owned = owned_sets(levels, gy)
    coupled = [piece for piece in range(len(pieces)) if pieces[piece][0] == 0]
    plain = [piece for piece in range(len(pieces)) if pieces[piece][0] > 0]
    section = lax.axis_index("comp")
    g = lax.axis_index("gx")
    h = lax.axis_index("gy")
    me = g * gy + h
    sides = ((g + gx - 1) % gx, (g + 1) % gx)
    ends = (0, rows - 1)
    masks = far_first(gy)
    leaving = []

    def load(source, target, at):
        copy = pltpu.make_async_copy(source, target, load_sem.at[at])
        copy.start()
        return copy

    load_high = load(state_hbm.at[pl.ds(FC, levels - FC)], fields.at[pl.ds(FC, levels - FC)], 0)
    load_low = load(state_hbm.at[pl.ds(0, FC)], fields.at[pl.ds(0, FC)], 1)

    load_dst = load(dst_hbm, dst_ref, 5)

    barrier = pltpu.get_barrier_semaphore()

    def greet(**device):
        pl.semaphore_signal(barrier, inc=1, device_id=device, device_id_type=MESH)

    for mask in masks:
        greet(gy=flipped(h, mask, gy))

    @pl.loop(0, peers)
    def _(q):
        greet(comp=1 - section, gx=q // gy, gy=q % gy)

    for side in sides:
        for mask in [*masks, 0]:
            greet(gx=side, gy=flipped(h, mask, gy))

    load_src = load(src_hbm, src_ref, 2)
    load_weight = load(weight_hbm, weight_ref, 3)
    load_count = load(count_hbm, count_ref, 4)

    def filled(tall, count):
        if count > tall.shape[0]:
            tall = jnp.concatenate([tall, jnp.zeros((count - tall.shape[0], LANES), F32)], axis=0)
        return tall

    def remote(source, target, send_sem, recv_sem, way=None, **device):
        copy = pltpu.make_async_remote_copy(
            src_ref=source,
            dst_ref=target,
            send_sem=send_sem,
            recv_sem=recv_sem,
            device_id=device,
            device_id_type=MESH,
        )
        if way is None:
            copy.start()
        else:
            copy = Guarded(copy, *((g > 0, g < gx - 1) if way == 0 else (g < gx - 1, g > 0)))
        leaving.append(copy)
        return copy

    def exchange(source, target, send_sem, recv_sem, j):
        copies = {}
        for mask in masks:
            other = flipped(h, mask, gy)
            copies[mask] = remote(
                source.at[j, other], target.at[j, h], send_sem.at[j, mask], recv_sem.at[j, mask], gy=other
            )
        target[j, h] = source[j, h]
        return copies

    def counts(piece):
        low, high = pieces[piece][:2]
        return range((high - low) // gy)

    def pack_piece(piece):
        low, _, first, count, _ = pieces[piece]
        for j in counts(piece):
            for owner in range(gy):
                values = fields[low + j * gy + owner, pl.ds(first, count), :]
                tall = jnp.concatenate([values[:, i * LANES : (i + 1) * LANES] for i in range(nb)], axis=0)
                fsend[piece][j, owner] = filled(tall, fsend[piece].shape[2]).astype(BF16)

    def send_forward(piece):
        return [exchange(fsend[piece], frecv[piece], fsend_sem[piece], frecv_sem[piece], j) for j in counts(piece)]

    def expand_gains():
        groups, width = LANES // 16, blocks * 16
        rows_all = []
        for low, many in owned:
            for j in range(many):
                line = resp[pl.ds(low + j * gy + h, 1), :] * np.float32(2.0 / (groups * width))
                rows_all.append(jnp.concatenate([line[:, i * width : (i + 1) * width] for i in range(groups)], axis=0))
        values = jnp.concatenate(rows_all, axis=0)
        count = values.shape[0]
        top = values.astype(BF16)
        rest = (values - top.astype(F32)).astype(BF16)
        both = jnp.concatenate([top, rest], axis=0)
        lane = lax.broadcasted_iota(jnp.int32, (groups, 2 * LANES), 1) % LANES
        mine = lane // 16 == lax.broadcasted_iota(jnp.int32, (groups, 2 * LANES), 0)
        for k in range(blocks // 2):
            span = pl.ds(k * 2 * LANES, 2 * LANES)
            wide = jnp.dot(both, place[:, span], preferred_element_type=F32)
            wide = wide[:count] + wide[count:]
            at = 0
            for which, (_, many) in enumerate(owned):
                for j in range(many):
                    mixed = jnp.where(mine, wide[at : at + groups], 0.0)
                    gains[which, j, :, span] = jnp.sum(mixed, axis=0, keepdims=True)
                    at += groups

    def transform(piece, arriving):
        _, _, first, count, which = pieces[piece]
        tallest = nb * count
        sent, early = [], []
        for j in counts(piece):
            for copy in arriving[j].values():
                copy.wait_recv()
            joins = piece in coupled and j == 0

            def coupling(source, i):
                return landed[source, pl.ds(i * rows + first, count), :]

            x = []
            for source in range(gy):
                tall = frecv[piece][j, source].astype(F32)[:tallest]
                for i in range(nb):
                    part = tall[i * count : (i + 1) * count]
                    x.append(part + coupling(source, i) if joins else part)
            p, q = block_forward(x)
            pz, qz = {}, {}
            for k in range(blocks // 2):
                one, two = (p[k], q[k]) if k else (p[0], p[blocks // 2])
                y = jnp.concatenate([one, two], axis=1).astype(BF16)
                spec = jnp.dot(y, table[k], preferred_element_type=F32)
                filtered = (spec * gains[which, j, :, pl.ds(k * 2 * LANES, 2 * LANES)]).astype(BF16)
                z = lax.dot_general(filtered, table[k], (((1,), (1,)), ((), ())), preferred_element_type=F32)
                pz[k] = z[:, :LANES]
                if k:
                    qz[k] = z[:, LANES:]
                else:
                    pz[blocks // 2] = z[:, LANES:]
            back = block_backward(pz, qz)
            if joins:
                back = [part + coupling(a // nb, a % nb) for a, part in enumerate(back)]
            for way, row in enumerate(ends):
                if first <= row < first + count:
                    for owner in range(gy):
                        parts = [part[row - first : row - first + 1] for part in back[owner * nb : (owner + 1) * nb]]
                        esend[which, way, j, owner] = filled(jnp.concatenate(parts, axis=0), 8).astype(BF16)
                    for mask in [*masks, 0]:
                        other = flipped(h, mask, gy)
                        early.append(remote(
                            esend.at[which, way, j, other], erecv.at[which, way, j, h],
                            esend_sem.at[which, way, j, mask], erecv_sem.at[which, way, j, mask],
                            way=way, gx=sides[way], gy=other,
                        ))
            for owner in range(gy):
                tall = jnp.concatenate(back[owner * nb : (owner + 1) * nb], axis=0)
                bsend[piece][j, owner] = filled(tall, bsend[piece].shape[2]).astype(BF16)
            sent.append(exchange(bsend[piece], brecv[piece], bsend_sem[piece], brecv_sem[piece], j))
        return sent, early

    def updated(piece, j, owner):
        low, _, first, count, _ = pieces[piece]
        tall = brecv[piece][j, owner].astype(F32)
        wide = jnp.concatenate([tall[i * count : (i + 1) * count] for i in range(nb)], axis=1)
        return fields[low + j * gy + owner, pl.ds(first, count), :] + wide

    def send_raw_edges():
        for level in range(levels):
            for way, row in enumerate(ends):
                edges[way, pl.ds(level, 1), :] = fields[level, pl.ds(row, 1), :]
        return [
            remote(edges.at[way], halos.at[way], hsend_sem.at[way], hrecv_sem.at[way], way=way, gx=sides[way])
            for way in range(2)
        ]

    def finish_level(which, j, owner, values):
        level = owned[which][0] + j * gy + owner
        row = lax.broadcasted_iota(jnp.int32, (rows, cols), 0)
        keep = jnp.where(section == 1, land[...].astype(F32), 1.0)
        above = jnp.where(g == gx - 1, 0.0, 1.0)
        below = jnp.where(g == 0, 0.0, 1.0)
        after, before = halos[0, pl.ds(level, 1), :], halos[1, pl.ds(level, 1), :]
        returned = [erecv[which, way, j, owner].astype(F32) for way in range(2)]
        wide = [jnp.concatenate([tall[i : i + 1] for i in range(nb)], axis=1) for tall in returned]
        after, before = after + wide[0], before + wide[1]
        after = jnp.where(row == rows - 1, after * above, pltpu.roll(values, rows - 1, 0))
        before = jnp.where(row == 0, before * below, pltpu.roll(values, 1, 0))
        out_ref[level] = (values + rate[...] * (after + before - 2.0 * values)) * keep

    def cells(index):
        row = ((index.astype(F32) + 0.5) * np.float32(1.0 / cols)).astype(jnp.int32)
        return row, index - row * cols

    def gather_couplings():
        wide = 2 * LANES if cols % (2 * LANES) == 0 else LANES
        parts = cols // wide
        chunk = gy * slots
        surface = jnp.concatenate(
            [fields[c, :, pl.ds(i * wide, wide)] for c in range(FC) for i in range(parts)], axis=0
        ).astype(BF16)

        @pl.loop(0, gx)
        def _(way):
            base = way * gy
            index = jnp.concatenate([src_ref[pl.ds(base + i, 1), :] for i in range(gy)], axis=1)
            row, col = cells(index)
            part = col // wide
            pick = jnp.where(lax.broadcasted_iota(jnp.int32, (wide, chunk), 0) == col - part * wide, 1.0, 0.0)
            found = jnp.dot(surface, pick.astype(BF16), preferred_element_type=F32).reshape(FC, parts * rows, chunk)
            mine = (lax.broadcasted_iota(jnp.int32, (parts * rows, chunk), 0) == part * rows + row)[None]
            values = jnp.sum(jnp.where(mine, found, 0.0), axis=1)
            scaled = []
            for i in range(gy):
                slot = lax.broadcasted_iota(jnp.int32, (1, slots), 1)
                weight = jnp.where(slot < count_ref[base + i], weight_ref[pl.ds(base + i, 1), :], 0.0)
                scaled.append(values[:, i * slots : (i + 1) * slots] * weight)
            for c in range(FC):
                sendc[way * FC + c] = jnp.concatenate([part[c : c + 1] for part in scaled], axis=0).astype(BF16)

    def couple_copy(target):
        return pltpu.make_async_remote_copy(
            src_ref=sendc.at[target],
            dst_ref=recvc.at[me],
            send_sem=csend_sem,
            recv_sem=crecv_sem,
            device_id={"comp": 1 - section, "gx": target // FC, "gy": target % FC},
            device_id_type=MESH,
        )

    couplings = pltpu.make_async_remote_copy(
        src_ref=sendc, dst_ref=recvc, send_sem=csend_sem, recv_sem=crecv_sem,
        device_id={"comp": 1 - section}, device_id_type=MESH,
    )

    def land_couplings():
        couplings.wait_recv()
        per = CHUNK // slots
        landing[...] = dsts[...].astype(jnp.int32)
        for source in range(gy):
            def chunk_sum(c, total):
                base = c * per
                index = jnp.concatenate([landing[source, pl.ds(base + i, 1), :] for i in range(per)], axis=1)
                values = [recvc[base + i].astype(F32)[source : source + 1] for i in range(per)]
                values = jnp.concatenate(values, axis=1)
                row, col = cells(index)
                block = col // LANES
                mine = lax.broadcasted_iota(jnp.int32, (lines, CHUNK), 0) == block * rows + row
                lane = lax.broadcasted_iota(jnp.int32, (LANES, CHUNK), 0) == col - block * LANES
                return total + lax.dot_general(
                    jnp.where(mine, 1.0, 0.0).astype(BF16),
                    jnp.where(lane, values, 0.0).astype(BF16),
                    (((1,), (1,)), ((), ())),
                    preferred_element_type=F32,
                )

            landed[source] = lax.fori_loop(
                0, peers // per, chunk_sum, jnp.zeros((lines, LANES), F32), unroll=min(8, peers // per)
            )

    for way, border in enumerate((gx - 1, 0)):
        @pl.when(g == border)
        def _(way=way):
            halos[way] = jnp.zeros(halos.shape[1:], F32)
            erecv[:, way] = jnp.zeros((erecv.shape[0], *erecv.shape[2:]), BF16)

    forward, backward = {}, {}
    load_high.wait()
    for piece in plain:
        pack_piece(piece)
    load_low.wait()
    for load_one in (load_src, load_weight, load_count):
        load_one.wait()
    gather_couplings()
    for piece in coupled:
        pack_piece(piece)
    load_dst.wait()
    short[...] = dst_ref[...].astype(jnp.int16)
    pl.semaphore_wait(barrier, gy - 1 + peers + 2 * gy)
    indices = []
    for mask in masks:
        other = flipped(h, mask, gy)
        indices.append(remote(short, dsts.at[h], isend_sem.at[mask], irecv_sem.at[mask], gy=other))
    dsts[h] = short[...]

    @pl.loop(0, gx * FC)
    def _(target):
        couple_copy(target).start()

    for piece in plain:
        forward[piece] = send_forward(piece)
    for piece in coupled:
        forward[piece] = send_forward(piece)
    halo = send_raw_edges()
    load_place = load(place_hbm, place, 6)
    load_resp = load(resp_hbm, resp, 7)
    load_table = load(table_hbm, table, 8)
    load_rate = load(rate_hbm, rate, 9)
    load_land = load(land_hbm, land, 10)
    load_place.wait()
    load_resp.wait()
    expand_gains()
    load_table.wait()
    for piece in plain:
        backward[piece] = transform(piece, forward[piece])
    for copy in indices:
        copy.wait_recv()
    if FC == gy:
        land_couplings()
    else:
        pl.when(h < FC)(land_couplings)

        @pl.when(h >= FC)
        def _():
            landed[...] = jnp.zeros_like(landed)

    settled = len(leaving)
    for piece in coupled:
        backward[piece] = transform(piece, forward[piece])
    load_rate.wait()
    load_land.wait()
    for copy in halo:
        copy.wait_recv()
    for which in range(len(owned)):
        group = [piece for piece in range(len(pieces)) if pieces[piece][4] == which]
        if coupled[0] in group:
            couplings.wait_send()
            for copy in leaving[:settled]:
                copy.wait_send()
        for piece in group:
            for copy in backward[piece][1]:
                copy.wait_recv()
        for j in counts(group[0]):
            for mask in [0, *reversed(masks)]:
                owner = flipped(h, mask, gy)
                for piece in group:
                    if mask:
                        backward[piece][0][j][mask].wait_recv()
                finish_level(which, j, owner, jnp.concatenate([updated(piece, j, owner) for piece in group], axis=0))
    for copy in leaving[settled:]:
        copy.wait_send()


def local(state, response, diffusion, land_mask, couple_src, couple_dst, couple_weight, couple_count):
    levels, rows, cols = state.shape[1:]
    gx, gy = lax.axis_size("gx"), lax.axis_size("gy")
    peers, slots = couple_src.shape[3:]
    cols_all = cols * gy
    nb, blocks = cols // LANES, cols_all // LANES
    lines = nb * rows
    pieces = phases(levels, rows, gy)
    owned = owned_sets(levels, gy)
    many = max(count for _, count in owned)
    tables = jnp.asarray(lane_tables(cols_all))
    places = jnp.asarray(spread_table(blocks))
    hbm = pl.BlockSpec(memory_space=pltpu.HBM)
    stay = lambda value: pltpu.with_memory_space_constraint(value, pltpu.HBM)
    dma = pltpu.SemaphoreType.DMA
    messages = [
        ((high - low) // gy, gy, -(-(nb * count) // 16) * 16, LANES) for low, high, _, count, _ in pieces
    ]
    out = pl.pallas_call(
        functools.partial(kernel, gx, gy, pieces),
        out_shape=jax.ShapeDtypeStruct((levels, rows, cols), F32),
        in_specs=[hbm] * 10,
        out_specs=pl.BlockSpec(memory_space=pltpu.VMEM),
        scratch_shapes=[
            pltpu.VMEM((levels, rows, cols), F32),
            pltpu.VMEM(tables.shape, BF16),
            pltpu.VMEM(places.shape, BF16),
            pltpu.VMEM((levels, cols_all), F32),
            pltpu.VMEM((len(owned), many, 1, cols_all), F32),
            pltpu.VMEM((rows, cols), F32),
            pltpu.VMEM((rows, cols), jnp.int32),
            pltpu.VMEM((peers, slots), jnp.int32),
            pltpu.VMEM((peers, slots), jnp.int32),
            pltpu.VMEM((peers, slots), F32),
            pltpu.SMEM((peers,), jnp.int32),
            pltpu.VMEM((gx * FC, gy, slots), BF16),
            pltpu.VMEM((peers, gy, slots), BF16),
            pltpu.VMEM((peers, slots), jnp.int16),
            pltpu.VMEM((gy, peers, slots), jnp.int16),
            pltpu.VMEM((gy, peers, slots), jnp.int32),
            pltpu.VMEM((gy, lines, LANES), F32),
            pltpu.VMEM((len(owned), 2, many, gy, 8, LANES), BF16),
            pltpu.VMEM((len(owned), 2, many, gy, 8, LANES), BF16),
            pltpu.VMEM((2, levels, cols), F32),
            pltpu.VMEM((2, levels, cols), F32),
            dma((11,)),
            dma,
            dma,
            dma((gy,)),
            dma((gy,)),
            dma((len(owned), 2, many, gy)),
            dma((len(owned), 2, many, gy)),
            dma((2,)),
            dma((2,)),
            *[pltpu.VMEM(message, BF16) for _ in range(4) for message in messages],
            *[dma(message[:2]) for _ in range(4) for message in messages],
        ],
        compiler_params=pltpu.CompilerParams(
            collective_id=0, has_side_effects=True, vmem_limit_bytes=48 * 1024 * 1024
        ),
    )(
        *map(
            stay,
            (
                state[0],
                response[0],
                diffusion[0],
                land_mask,
                couple_src.reshape(peers, slots),
                couple_dst.reshape(peers, slots),
                couple_weight.reshape(peers, slots),
                couple_count.reshape(peers),
                tables,
                places,
            ),
        )
    )
    return out[None]


def solution(mesh):
    return jax.shard_map(
        local,
        mesh=mesh,
        in_specs=(
            P("comp", None, "gx", "gy"),
            P("comp", None, None),
            P("comp", "gx", "gy"),
            P("gx", "gy"),
            P("comp", "gx", "gy", None, None),
            P("comp", "gx", "gy", None, None),
            P("comp", "gx", "gy", None, None),
            P("comp", "gx", "gy", None),
        ),
        out_specs=P("comp", None, "gx", "gy"),
        check_vma=False,
    )
```
